128 devices in a mesh: sec: 4 (over z_lo, core), lat: 32 (over x, z_hi, y).
Axes of the slice: x: 4, y: 4, z: 4 (z_hi: 2, z_lo: 2; z = z_hi * 2 + z_lo), core: 2. Of those that a mesh axis runs over, the one named last changes fastest.
Arguments:
- ocean_state: float32 [24, 512, 1024], P(None, 'lat', 'sec'), may hold values from -6 to 6
- land_mask: int32 [512, 1024], P('lat', 'sec'), may hold values from 0 to 1
- layer_count: int32 [512, 1024], P('lat', 'sec'), may hold values from 1 to 8
- conv1_weight: bfloat16 [5, 128, 120], replicated, may hold values from -1 to 1
- conv1_bias: float32 [128], replicated, may hold values from -3 to 3
- conv2_weight: bfloat16 [5, 64, 640], replicated, may hold values from -1 to 1
- conv2_bias: float32 [64], replicated, may hold values from -3 to 3
- conv3_weight: bfloat16 [5, 32, 320], replicated, may hold values from -1 to 1
- conv3_bias: float32 [32], replicated, may hold values from -3 to 3
- conv4_weight: bfloat16 [5, 16, 160], replicated, may hold values from -1 to 1
Outputs:
- final_state: float32 [24, 512, 1024], P(None, 'lat', 'sec')
- forcing: float32 [16, 512, 1024], P(None, 'lat', 'sec')
The draws below stay inside these ranges and needn't reach their ends.
All inputs are finite; a program needn't handle non-finite values.
Results may differ from the reference program's by a relative error of at most 0.015.
Values may be sent and summed in bfloat16 or wider, within the bound.
No kernel may reach another device: no remote copies, remote signals or barrier semaphores. Data moves between devices by JAX's collectives and lax.ppermute only.
A program may use at most 128 MiB of HBM per device.

```python
import jax
import jax.numpy as jnp
from jax import lax

LEVELS = 8
CIN = 24
COUT = 16
H1 = 128
H2 = 64
H3 = 32
STEPS = 4
NY = 512
NX = 1024


def basin_parts(key):
    basin_size = min(NY, NX)
    row_index = lax.broadcasted_iota(jnp.int32, (NY, NX), 0)
    col_index = lax.broadcasted_iota(jnp.int32, (NY, NX), 1)
    centre_rows = jax.random.randint(jax.random.fold_in(key, 11), (8,), 0, NY)
    centre_cols = jax.random.randint(jax.random.fold_in(key, 12), (8,), 0, NX)
    least_radius = max(basin_size // 16, 1)
    radius_all = jax.random.randint(jax.random.fold_in(key, 13), (8,), least_radius, max(basin_size // 4, least_radius + 1))
    shore_gap = jnp.full((NY, NX), 2 ** 30, jnp.int32)
    for continent in range(8):
        row_gap = row_index - centre_rows[continent]
        col_gap = col_index - centre_cols[continent]
        excess = row_gap * row_gap + col_gap * col_gap - radius_all[continent] * radius_all[continent]
        shore_gap = jnp.minimum(shore_gap, excess)
    return (row_index, col_index, shore_gap)


def draw_land_mask(key, part):
    row_index, col_index, shore_gap = basin_parts(jax.random.fold_in(key, 5))
    sea_cells = (shore_gap > 0).astype(jnp.int32)
    corner = (row_index == 0) & (col_index == 0)
    return jnp.where(corner, 1, sea_cells).astype(jnp.int32)


def draw_layer_count(key, part):
    row_index, col_index, shore_gap = basin_parts(jax.random.fold_in(key, 5))
    basin_size = min(NY, NX)
    least_cycle = max(basin_size * basin_size // 256, 1)
    cycle_width = jax.random.randint(jax.random.fold_in(key, 6), (), least_cycle, max(basin_size * basin_size // 16, least_cycle + 1))
    depth_count = jnp.ones((NY, NX), jnp.int32)
    for cycle_number in range(1, LEVELS):
        depth_count = depth_count + (shore_gap > cycle_number * cycle_width).astype(jnp.int32)
    jitter = jax.random.randint(jax.random.fold_in(key, 7), (NY, NX), -1, 2)
    depth_count = jnp.clip(depth_count + jitter, 1, LEVELS)
    depth_count = jnp.where((row_index == 0) & (col_index == 0), LEVELS, depth_count)
    depth_count = jnp.where((row_index == 0) & (col_index == 1), 1, depth_count)
    return depth_count.astype(jnp.int32)


def draw_ocean_state(key, part):
    magnitude = jax.random.uniform(jax.random.fold_in(key, 61), (2 * LEVELS, 1, 1), jnp.float32, 1.5, 2.5)
    flips = jax.random.randint(jax.random.fold_in(key, 62), (2 * LEVELS, 1, 1), 0, 2)
    offset_vel = magnitude * (2 * flips - 1).astype(jnp.float32)
    drift = jnp.concatenate([offset_vel, jnp.zeros((LEVELS, 1, 1), jnp.float32)], axis=0)
    noise = jnp.clip(jax.random.normal(jax.random.fold_in(key, 64), (CIN, NY, NX), jnp.float32), -3.5, 3.5)
    return (noise + drift).astype(jnp.float32)


def kernel_taps(key, out_width, in_width):
    spread = (25.0 * in_width) ** (-0.5)
    taps = jnp.clip(jax.random.normal(jax.random.fold_in(key, 21), (5, out_width, 5, in_width), jnp.float32), -4.0, 4.0)
    common = jnp.clip(jax.random.normal(jax.random.fold_in(key, 22), (1, out_width, 1, in_width), jnp.float32), -3.0, 3.0)
    weight = spread * (taps + 0.35 * common)
    return weight.reshape(5, out_width, 5 * in_width).astype(jnp.bfloat16)


def draw_conv1_weight(key, part):
    return kernel_taps(jax.random.fold_in(key, 31), H1, CIN)


def draw_conv2_weight(key, part):
    return kernel_taps(jax.random.fold_in(key, 41), H2, H1)


def draw_conv3_weight(key, part):
    return kernel_taps(jax.random.fold_in(key, 51), H3, H2)


def draw_conv4_weight(key, part):
    return kernel_taps(jax.random.fold_in(key, 71), COUT, H3)


def gaussian(key, extent, scale, bound, held_as=jnp.bfloat16):
    return jnp.clip(scale * jax.random.normal(key, extent, jnp.float32), -bound, bound).astype(held_as)


def setup_inputs(seed: int = 0) -> dict:
    key_list = jax.random.split(jax.random.key(seed), 11)
    ocean_state = draw_ocean_state(jax.random.fold_in(key_list[10], 71), 0)
    land_mask = draw_land_mask(jax.random.fold_in(key_list[10], 71), 0)
    layer_count = draw_layer_count(jax.random.fold_in(key_list[10], 71), 0)
    conv1_weight = draw_conv1_weight(jax.random.fold_in(key_list[10], 71), 0)
    conv1_bias = gaussian(key_list[4], (H1,), 0.5, 3.0, jnp.float32)
    conv2_weight = draw_conv2_weight(jax.random.fold_in(key_list[10], 71), 0)
    conv2_bias = gaussian(key_list[6], (H2,), 0.5, 3.0, jnp.float32)
    conv3_weight = draw_conv3_weight(jax.random.fold_in(key_list[10], 71), 0)
    conv3_bias = gaussian(key_list[8], (H3,), 0.5, 3.0, jnp.float32)
    conv4_weight = draw_conv4_weight(jax.random.fold_in(key_list[10], 71), 0)
    return {"ocean_state": ocean_state, "land_mask": land_mask, "layer_count": layer_count, "conv1_weight": conv1_weight, "conv1_bias": conv1_bias, "conv2_weight": conv2_weight, "conv2_bias": conv2_bias, "conv3_weight": conv3_weight, "conv3_bias": conv3_bias, "conv4_weight": conv4_weight}


time_step = 0.3
drag_rate = 0.05


def coupling(count_levels):
    row_index = lax.broadcasted_iota(jnp.int32, (count_levels, count_levels), 0)
    col_index = lax.broadcasted_iota(jnp.int32, (count_levels, count_levels), 1)
    return 0.5 + 0.1 * jnp.minimum(row_index, col_index).astype(jnp.float32)


def conv_layer(layer_in, weight):
    out_rows = layer_in.shape[1] - 4
    out_cols = layer_in.shape[2] - 4
    summed = jnp.zeros((weight.shape[1], out_rows, out_cols), jnp.float32)
    for shift_y in range(5):
        row_band = layer_in[:, shift_y:shift_y + out_rows, :]
        stacked = jnp.concatenate([row_band[:, :, shift_x:shift_x + out_cols] for shift_x in range(5)], axis=0)
        summed = summed + jnp.einsum("oc,crx->orx", weight[shift_y], stacked, preferred_element_type=jnp.float32)
    return summed


def ocean_step(padded, wet_pad, forcing, coriolis, coupling_matrix):
    zonal_vel = padded[:LEVELS]
    merid_vel = padded[LEVELS:2 * LEVELS]
    thickness = padded[2 * LEVELS:]
    divergence = (zonal_vel[:, 1:-1, 2:] - zonal_vel[:, 1:-1, :-2]) * 0.5 + (merid_vel[:, 2:, 1:-1] - merid_vel[:, :-2, 1:-1]) * 0.5
    h_cycle = (thickness[:, 1:-1, 1:-1] - time_step * divergence) * wet_pad[:, 1:-1, 1:-1]
    pressure = jnp.einsum("kj,jrx->krx", coupling_matrix, h_cycle, precision=lax.Precision.HIGHEST)
    grad_x = (pressure[:, 1:-1, 2:] - pressure[:, 1:-1, :-2]) * 0.5
    grad_y = (pressure[:, 2:, 1:-1] - pressure[:, :-2, 1:-1]) * 0.5
    zonal_mid = zonal_vel[:, 2:-2, 2:-2]
    merid_mid = merid_vel[:, 2:-2, 2:-2]
    wet_mid = wet_pad[:, 2:-2, 2:-2]
    zonal_new = (zonal_mid + time_step * (-grad_x + coriolis * merid_mid - drag_rate * zonal_mid + forcing[:LEVELS])) * wet_mid
    merid_new = (merid_mid + time_step * (-grad_y - coriolis * zonal_mid - drag_rate * merid_mid + forcing[LEVELS:])) * wet_mid
    return jnp.concatenate([zonal_new, merid_new, h_cycle[:, 1:-1, 1:-1]], axis=0)


def pad_two(field):
    return jnp.pad(field, ((0, 0), (2, 2), (2, 2)))


def reference(ocean_state, land_mask, layer_count, conv1_weight, conv1_bias, conv2_weight, conv2_bias, conv3_weight, conv3_bias, conv4_weight):
    levels = land_mask * layer_count
    wet_mask = (lax.broadcasted_iota(jnp.int32, (LEVELS, NY, NX), 0) < levels[None]).astype(jnp.float32)
    sea_mask = (levels > 0).astype(jnp.float32)[None]
    wet_two = jnp.concatenate([wet_mask, wet_mask], axis=0)
    wet_three = jnp.concatenate([wet_mask, wet_mask, wet_mask], axis=0)
    counts = jnp.maximum(jnp.sum(wet_mask, axis=(1, 2)), 1.0)
    counts_two = jnp.concatenate([counts, counts])
    coriolis = 0.3 + 0.5 * lax.broadcasted_iota(jnp.int32, (1, NY, 1), 1).astype(jnp.float32) / NY
    coupling_matrix = coupling(LEVELS)
    state = ocean_state * wet_three
    forcing = jnp.zeros((2 * LEVELS, NY, NX), jnp.float32)
    for step_index in range(STEPS):
        hidden = state.astype(jnp.bfloat16)
        for weight, offset in ((conv1_weight, conv1_bias), (conv2_weight, conv2_bias), (conv3_weight, conv3_bias)):
            hidden = (jax.nn.silu(conv_layer(pad_two(hidden), weight) + offset[:, None, None]) * sea_mask).astype(jnp.bfloat16)
        raw_forcing = conv_layer(pad_two(hidden), conv4_weight)
        wet_sums = jnp.sum(raw_forcing * wet_two, axis=(1, 2))
        forcing = (raw_forcing - (wet_sums / counts_two)[:, None, None]) * wet_two
        state = ocean_step(pad_two(state), pad_two(wet_mask), forcing, coriolis, coupling_matrix)
    return state, forcing
```

```python
import jax
import jax.numpy as jnp
from jax import lax
from jax.sharding import PartitionSpec as P

LEVELS = 8
STEPS = 4


time_step = 0.3
drag_rate = 0.05


def padded_2(block, sides, width):
    for axis, dim in sides:
        count = lax.axis_size(axis)
        forward = [(i, i + 1) for i in range(count - 1)]
        backward = [(target, source) for source, target in forward]
        low = lax.ppermute(
            lax.slice_in_dim(block, block.shape[dim] - width, None, axis=dim), axis, forward
        )
        high = lax.ppermute(lax.slice_in_dim(block, 0, width, axis=dim), axis, backward)
        block = jnp.concatenate([low, block, high], axis=dim)
    return block


def total(values):
    count = lax.axis_size("sec") * lax.axis_size("lat")
    width = values.shape[0]
    row = jnp.pad(values, (0, 128 - width))
    copies = jnp.broadcast_to(row[None, None, :], (count, 1, 128))
    received = lax.all_to_all(copies, ("sec", "lat"), 0, 0)
    return jnp.sum(received, axis=(0, 1))[:width]


def coupling(count_levels):
    row_index = lax.broadcasted_iota(jnp.int32, (count_levels, count_levels), 0)
    col_index = lax.broadcasted_iota(jnp.int32, (count_levels, count_levels), 1)
    return 0.5 + 0.1 * jnp.minimum(row_index, col_index).astype(jnp.float32)


def conv_layer(layer_in, weight):
    out_rows = layer_in.shape[1] - 4
    out_cols = layer_in.shape[2] - 4
    summed = jnp.zeros((weight.shape[1], out_rows, out_cols), jnp.float32)
    for shift_y in range(5):
        row_band = layer_in[:, shift_y : shift_y + out_rows, :]
        stacked = jnp.concatenate(
            [row_band[:, :, shift_x : shift_x + out_cols] for shift_x in range(5)], axis=0
        )
        summed = summed + jnp.einsum(
            "oc,crx->orx", weight[shift_y], stacked, preferred_element_type=jnp.float32
        )
    return summed


def ocean_step(padded, wet_pad, forcing, coriolis, coupling_matrix):
    zonal_vel = padded[:LEVELS]
    merid_vel = padded[LEVELS : 2 * LEVELS]
    thickness = padded[2 * LEVELS :]
    divergence = (zonal_vel[:, 1:-1, 2:] - zonal_vel[:, 1:-1, :-2]) * 0.5 + (
        merid_vel[:, 2:, 1:-1] - merid_vel[:, :-2, 1:-1]
    ) * 0.5
    h_cycle = (thickness[:, 1:-1, 1:-1] - time_step * divergence) * wet_pad[:, 1:-1, 1:-1]
    pressure = jnp.einsum("kj,jrx->krx", coupling_matrix, h_cycle, precision=lax.Precision.HIGHEST)
    grad_x = (pressure[:, 1:-1, 2:] - pressure[:, 1:-1, :-2]) * 0.5
    grad_y = (pressure[:, 2:, 1:-1] - pressure[:, :-2, 1:-1]) * 0.5
    zonal_mid = zonal_vel[:, 2:-2, 2:-2]
    merid_mid = merid_vel[:, 2:-2, 2:-2]
    wet_mid = wet_pad[:, 2:-2, 2:-2]
    zonal_new = (
        zonal_mid
        + time_step * (-grad_x + coriolis * merid_mid - drag_rate * zonal_mid + forcing[:LEVELS])
    ) * wet_mid
    merid_new = (
        merid_mid
        + time_step * (-grad_y - coriolis * zonal_mid - drag_rate * merid_mid + forcing[LEVELS:])
    ) * wet_mid
    return jnp.concatenate([zonal_new, merid_new, h_cycle[:, 1:-1, 1:-1]], axis=0)


def local(
    ocean_state,
    land_mask,
    layer_count,
    conv1_weight,
    conv1_bias,
    conv2_weight,
    conv2_bias,
    conv3_weight,
    conv3_bias,
    conv4_weight,
):
    dev_rows = ocean_state.shape[1]
    dev_cols = ocean_state.shape[2]
    row_start = lax.axis_index("lat") * dev_rows
    grid_rows = lax.axis_size("lat") * dev_rows
    levels = land_mask * layer_count
    levels_ext = padded_2(levels, (("sec", 1), ("lat", 0)), 8)
    wet_ext = (
        lax.broadcasted_iota(jnp.int32, (LEVELS, dev_rows + 16, dev_cols + 16), 0)
        < levels_ext[None]
    ).astype(jnp.float32)
    sea_ext = (levels_ext > 0).astype(jnp.float32)[None]
    wet_mask = wet_ext[:, 8:-8, 8:-8]
    wet_cycle = wet_ext[:, 6:-6, 6:-6]
    wet_two = jnp.concatenate([wet_mask, wet_mask], axis=0)
    wet_three = jnp.concatenate([wet_mask, wet_mask, wet_mask], axis=0)
    counts_two = None
    global_rows = row_start + lax.broadcasted_iota(jnp.int32, (1, dev_rows, 1), 1)
    coriolis = 0.3 + 0.5 * global_rows.astype(jnp.float32) / grid_rows
    coupling_matrix = coupling(LEVELS)
    state = ocean_state * wet_three
    forcing = jnp.zeros((2 * LEVELS, dev_rows, dev_cols), jnp.float32)
    for step_index in range(STEPS):
        net_in = padded_2(state.astype(jnp.bfloat16), (("sec", 2), ("lat", 1)), 8)
        ocean_in = net_in[:, 6:-6, 6:-6].astype(state.dtype)
        hidden = net_in
        for weight, offset, margin in (
            (conv1_weight, conv1_bias, 6),
            (conv2_weight, conv2_bias, 4),
            (conv3_weight, conv3_bias, 2),
        ):
            activation = jax.nn.silu(conv_layer(hidden, weight) + offset[:, None, None])
            sea_part = sea_ext[
                :, 8 - margin : 8 + dev_rows + margin, 8 - margin : 8 + dev_cols + margin
            ]
            hidden = (activation * sea_part).astype(jnp.bfloat16)
        raw_forcing = conv_layer(hidden, conv4_weight)
        wet_sums = jnp.sum(raw_forcing * wet_two, axis=(1, 2))
        if counts_two is None:
            both = total(jnp.concatenate([wet_sums, jnp.sum(wet_mask, axis=(1, 2))]))
            wet_sums = both[: 2 * LEVELS]
            counts = jnp.maximum(both[2 * LEVELS :], 1.0)
            counts_two = jnp.concatenate([counts, counts])
        else:
            wet_sums = total(wet_sums)
        forcing = (raw_forcing - (wet_sums / counts_two)[:, None, None]) * wet_two
        state = ocean_step(ocean_in, wet_cycle, forcing, coriolis, coupling_matrix)
    return (state, forcing)


def solution(mesh):
    return jax.shard_map(
        local,
        mesh=mesh,
        in_specs=(
            P(None, "lat", "sec"),
            P("lat", "sec"),
            P("lat", "sec"),
            P(),
            P(),
            P(),
            P(),
            P(),
            P(),
            P(),
        ),
        out_specs=(P(None, "lat", "sec"), P(None, "lat", "sec")),
        check_vma=False,
    )
```

```python
import functools

import jax
import jax.numpy as jnp
from jax import lax
from jax.experimental import pallas as pl
from jax.experimental.pallas import tpu as pltpu
from jax.sharding import PartitionSpec as P

LEVELS = 8
STEPS = 4
HALO = 8
TIME_STEP = 0.3
DRAG = 0.05
ROWS = 16
COLS = 256
EXT_ROWS = ROWS + 2 * HALO
WIDE = COLS + 128
SPAN = COLS + 2 * HALO
F32 = jnp.float32
BF16 = jnp.bfloat16


def banded(weight, in_pad, out_pad):
    out_width = weight.shape[1]
    in_width = weight.shape[2] // 5
    taps = weight.reshape(5, out_width, 5, in_width).transpose(2, 0, 3, 1)
    taps = jnp.pad(taps, ((0, 0), (0, 0), (0, in_pad - in_width), (0, 0)))
    bands = [jnp.pad(taps, ((0, 0), (j, 3 - j), (0, 0), (0, 0))) for j in range(4)]
    band = jnp.concatenate(bands, axis=3)
    halves = [
        band[:, 4 * i : 4 * i + 4].reshape(5 * 4 * in_pad, 4 * out_width) for i in range(2)
    ]
    full = jnp.concatenate(halves, axis=0)
    return jnp.pad(full, ((0, 0), (0, out_pad - 4 * out_width)))


def conv_rows(in_ref, weight_ref, group, count):
    lhs = jnp.concatenate([in_ref[group, 0:count, :], in_ref[group + 1, 0:count, :]], axis=1)
    return jnp.dot(lhs, weight_ref[...], preferred_element_type=F32)


def spread(value, work_ref, out_ref, group, width):
    work_ref[0:SPAN, 0:width] = value
    for shift in range(5):
        out_ref[group, :, shift * width : (shift + 1) * width] = work_ref[
            shift : shift + SPAN, 0:width
        ].astype(BF16)


def conv_layer(in_ref, weight_ref, bias_ref, sea_ref, work_ref, out_ref, layer, groups):
    width = weight_ref.shape[1]

    def body(group, carry):
        total = conv_rows(in_ref, weight_ref, group, SPAN)
        row_of = lax.broadcasted_iota(jnp.int32, (128, width), 0)
        lane_of = lax.broadcasted_iota(jnp.int32, (128, width), 1)
        wanted = 4 * group + 2 * (layer + 1) + lane_of // (width // 4)
        pick = jnp.where(row_of == wanted, 1.0, 0.0).astype(BF16)
        sea = jnp.dot(sea_ref[layer], pick, preferred_element_type=F32)
        biased = total + bias_ref[...]
        half = 0.5 * biased
        spread((half + half * jnp.tanh(half)) * sea, work_ref, out_ref, group, width)
        return carry

    lax.fori_loop(0, groups, body, 0)


def device_means(received):
    total = jnp.sum(received, axis=0, keepdims=True)
    column = jnp.transpose(jnp.broadcast_to(total, (128, 128)))
    counts = jnp.maximum(column[16:24], 1.0)
    return column[0:8] / counts, column[8:16] / counts


def step_kernel(*refs, first, last):
    refs = list(refs)
    start_ref = refs.pop(0)
    recv_ref = None if first else refs.pop(0)
    own_ref, left_ref, right_ref, top_ref, bottom_ref, wet_ref, sea_ref = refs[:7]
    w1_ref, w2_ref, w3_ref, w4_ref, b1_ref, b2_ref, b3_ref = refs[7:14]
    refs = refs[14:]
    new_ref = refs.pop(0)
    pay_ref = refs.pop(0)
    if last:
        raw_out_ref = refs.pop(0)
    else:
        send_left_ref = refs.pop(0)
        send_right_ref = refs.pop(0)
    state_ref, a0_ref, a1_ref, a2_ref, a3_ref, work_ref, raw_ref = refs

    lane = lax.broadcasted_iota(jnp.int32, (ROWS * 24, 128), 1)
    sides = jnp.where(lane < 64, right_ref[...].astype(F32), left_ref[...].astype(F32))
    state_ref[:, 24:32, :] = jnp.zeros((EXT_ROWS, 8, WIDE), F32)
    state_ref[HALO : HALO + ROWS, 0:24, 0:COLS] = own_ref[...]
    state_ref[HALO : HALO + ROWS, 0:24, COLS:WIDE] = sides.reshape(ROWS, 24, 128)
    state_ref[0:HALO, 0:24, :] = top_ref[...].astype(F32).reshape(HALO, 24, WIDE)
    state_ref[HALO + ROWS :, 0:24, :] = bottom_ref[...].astype(F32).reshape(HALO, 24, WIDE)
    if not first:
        zonal_mean, merid_mean = device_means(recv_ref[...])
        for base, mean in ((0, zonal_mean), (8, merid_mean)):
            scaled = jnp.concatenate([TIME_STEP * mean] * 3, axis=1)
            state_ref[:, base : base + 8, :] = (
                state_ref[:, base : base + 8, :] - scaled[None] * wet_ref[...]
            )

    work_ref[SPAN:, :] = jnp.zeros((8, 512), F32)
    for group in range(8):
        flat = state_ref[4 * group : 4 * group + 4].reshape(128, WIDE)
        turned = jnp.transpose(flat)
        spread(
            jnp.concatenate([turned[WIDE - HALO :], turned[0 : COLS + HALO]], axis=0),
            work_ref,
            a0_ref,
            group,
            128,
        )
    conv_layer(a0_ref, w1_ref, b1_ref, sea_ref, work_ref, a1_ref, 0, 7)
    conv_layer(a1_ref, w2_ref, b2_ref, sea_ref, work_ref, a2_ref, 1, 6)
    conv_layer(a2_ref, w3_ref, b3_ref, sea_ref, work_ref, a3_ref, 2, 5)
    for group in range(4):
        turned = jnp.transpose(conv_rows(a3_ref, w4_ref, group, COLS))
        raw_ref[4 * group : 4 * group + 4] = turned[0:64].reshape(4, 16, COLS)

    def shifted_difference(field):
        return (pltpu.roll(field, WIDE - 1, 2) - pltpu.roll(field, 1, 2)) * 0.5

    rows = ROWS + 2
    low = HALO - 1
    zonal = state_ref[low : low + rows, 0:8, :]
    merid_above = state_ref[low + 1 : low + 1 + rows, 8:16, :]
    merid_below = state_ref[low - 1 : low - 1 + rows, 8:16, :]
    divergence = shifted_difference(zonal) + (merid_above - merid_below) * 0.5
    thickness = state_ref[low : low + rows, 16:24, :]
    h_new = (thickness - TIME_STEP * divergence) * wet_ref[low : low + rows]
    level = lax.broadcasted_iota(jnp.int32, (1, 8, 1), 1)
    pressure = None
    for other in range(LEVELS):
        weight = 0.5 + 0.1 * jnp.minimum(level, other).astype(F32)
        term = weight * h_new[:, other : other + 1, :]
        pressure = term if pressure is None else pressure + term
    grad_x = shifted_difference(pressure[1:-1])[:, :, 0:COLS]
    grad_y = ((pressure[2:] - pressure[:-2]) * 0.5)[:, :, 0:COLS]
    wet = wet_ref[HALO : HALO + ROWS, :, 0:COLS]
    zonal_mid = state_ref[HALO : HALO + ROWS, 0:8, 0:COLS]
    merid_mid = state_ref[HALO : HALO + ROWS, 8:16, 0:COLS]
    global_row = start_ref[0] + lax.broadcasted_iota(jnp.int32, (ROWS, 8, COLS), 0)
    coriolis = 0.3 + 0.5 * global_row.astype(F32) / 512.0
    raw_zonal = raw_ref[:, 0:8, :]
    raw_merid = raw_ref[:, 8:16, :]
    zonal_new = (
        zonal_mid + TIME_STEP * (-grad_x + coriolis * merid_mid - DRAG * zonal_mid + raw_zonal)
    ) * wet
    merid_new = (
        merid_mid + TIME_STEP * (-grad_y - coriolis * zonal_mid - DRAG * merid_mid + raw_merid)
    ) * wet
    new_ref[:, 0:8, :] = zonal_new
    new_ref[:, 8:16, :] = merid_new
    new_ref[:, 16:24, :] = h_new[1:-1, :, 0:COLS]
    if last:
        raw_out_ref[...] = raw_ref[...]
    else:
        flat = new_ref[...].reshape(ROWS * 24, COLS).astype(BF16)
        send_left_ref[...] = flat[:, 0:128]
        send_right_ref[...] = flat[:, COLS - 128 :]

    def lanes_of(field):
        by_column = jnp.sum(field, axis=0)
        return by_column[:, 0:128] + by_column[:, 128:256]

    columns = jnp.concatenate(
        [
            lanes_of(raw_zonal * wet),
            lanes_of(raw_merid * wet),
            lanes_of(wet),
            jnp.zeros((104, 128), F32),
        ],
        axis=0,
    )
    row = jnp.sum(jnp.transpose(columns), axis=0, keepdims=True)
    pay_ref[...] = jnp.broadcast_to(row, (128, 128))


def ocean_network_step(first, last, args):
    n_vmem = len(args) - 1
    outs = [
        jax.ShapeDtypeStruct((ROWS, 24, COLS), F32),
        jax.ShapeDtypeStruct((128, 128), F32),
    ]
    if last:
        outs.append(jax.ShapeDtypeStruct((ROWS, 16, COLS), F32))
    else:
        outs += [jax.ShapeDtypeStruct((ROWS * 24, 128), BF16)] * 2
    vmem = pl.BlockSpec(memory_space=pltpu.VMEM)
    return pl.pallas_call(
        functools.partial(step_kernel, first=first, last=last),
        out_shape=outs,
        in_specs=[pl.BlockSpec(memory_space=pltpu.SMEM)] + [vmem] * n_vmem,
        out_specs=[vmem] * len(outs),
        scratch_shapes=[
            pltpu.VMEM((EXT_ROWS, 32, WIDE), F32),
            pltpu.VMEM((8, SPAN, 5 * 128), BF16),
            pltpu.VMEM((7, SPAN, 5 * 512), BF16),
            pltpu.VMEM((6, SPAN, 5 * 256), BF16),
            pltpu.VMEM((5, SPAN, 5 * 128), BF16),
            pltpu.VMEM((SPAN + 8, 512), F32),
            pltpu.VMEM((ROWS, 16, COLS), F32),
        ],
        name="last_step" if last else ("first_step" if first else "middle_step"),
    )(*args)


def finish_kernel(recv_ref, state_ref, raw_ref, wet_ref, final_ref, forcing_ref):
    zonal_mean, merid_mean = device_means(recv_ref[...])
    wet = wet_ref[HALO : HALO + ROWS, :, 0:COLS]
    zonal_mean = jnp.concatenate([zonal_mean] * 2, axis=1)[None]
    merid_mean = jnp.concatenate([merid_mean] * 2, axis=1)[None]
    forcing_ref[:, 0:8, :] = (raw_ref[:, 0:8, :] - zonal_mean) * wet
    forcing_ref[:, 8:16, :] = (raw_ref[:, 8:16, :] - merid_mean) * wet
    final_ref[:, 0:8, :] = state_ref[:, 0:8, :] - TIME_STEP * zonal_mean * wet
    final_ref[:, 8:16, :] = state_ref[:, 8:16, :] - TIME_STEP * merid_mean * wet
    final_ref[:, 16:24, :] = state_ref[:, 16:24, :]


def finish(received, state, raw, wet):
    return pl.pallas_call(
        finish_kernel,
        out_shape=[
            jax.ShapeDtypeStruct((ROWS, 24, COLS), F32),
            jax.ShapeDtypeStruct((ROWS, 16, COLS), F32),
        ],
        name="finish",
    )(received, state, raw, wet)


def exchange(send_left, send_right):
    def both_ways(axis, up, down):
        count = lax.axis_size(axis)
        forward = [(i, i + 1) for i in range(count - 1)]
        backward = [(target, source) for source, target in forward]
        return lax.ppermute(up, axis, forward), lax.ppermute(down, axis, backward)

    left, right = both_ways("sec", send_right, send_left)
    height = send_left.shape[0] // 2
    lane = lax.broadcasted_iota(jnp.int32, left.shape, 1)
    sides = jnp.where(lane < 64, right, left)
    whole = jnp.concatenate([send_left, send_right, sides], axis=1)
    top, bottom = both_ways("lat", whole[height:], whole[:height])
    return left, right, top, bottom


def local(
    ocean_state,
    land_mask,
    layer_count,
    conv1_weight,
    conv1_bias,
    conv2_weight,
    conv2_bias,
    conv3_weight,
    conv3_bias,
    conv4_weight,
):
    levels = land_mask * layer_count
    level_of = lax.broadcasted_iota(jnp.int32, (ROWS, LEVELS, COLS), 1)
    wet_own = (level_of < levels[:, None, :]).astype(F32)
    state = ocean_state.transpose(1, 0, 2) * jnp.concatenate([wet_own] * 3, axis=1)
    packed = jnp.concatenate(
        [state.astype(BF16), levels.astype(BF16)[:, None, :], jnp.zeros((ROWS, 7, COLS), BF16)],
        axis=1,
    ).reshape(ROWS * 32, COLS)
    parts = exchange(packed[:, :128], packed[:, 128:])
    left, right, top, bottom = [part.reshape(-1, 32, part.shape[1]) for part in parts]
    lane = lax.broadcasted_iota(jnp.int32, (1, 128), 1)
    middle = jnp.concatenate(
        [levels.astype(BF16), jnp.where(lane < 64, right[:, 24], left[:, 24])], axis=1
    )
    levels_ext = jnp.concatenate([top[:, 24], middle, bottom[:, 24]], axis=0).astype(F32)
    level_ext_of = lax.broadcasted_iota(jnp.int32, (EXT_ROWS, LEVELS, WIDE), 1).astype(F32)
    wet = (level_ext_of < levels_ext[:, None, :]).astype(F32)
    sea_turned = jnp.roll((levels_ext > 0).astype(BF16).T, HALO, axis=0)
    sea_turned = jnp.pad(sea_turned, ((0, 0), (0, 128 - EXT_ROWS)))
    sea = jnp.stack([sea_turned[shift : shift + SPAN] for shift in (2, 4, 6)])
    halos = [
        part[:, :24].reshape(-1, part.shape[2]) for part in (left, right, top, bottom)
    ]

    weights = [
        banded(conv1_weight, 32, 512),
        banded(conv2_weight, 128, 256),
        banded(conv3_weight, 64, 128),
        banded(conv4_weight, 32, 128),
        jnp.tile(conv1_bias, 4)[None],
        jnp.tile(conv2_bias, 4)[None],
        jnp.tile(conv3_bias, 4)[None],
    ]
    start = (lax.axis_index("lat") * ROWS).astype(jnp.int32)[None]
    received = []
    for step_index in range(STEPS):
        last = step_index == STEPS - 1
        results = ocean_network_step(
            step_index == 0, last, [start, *received, state, *halos, wet, sea, *weights]
        )
        state = results[0]
        if not last:
            halos = exchange(results[2], results[3])
        received = [lax.all_to_all(results[1], ("sec", "lat"), 0, 0)]
    final_state, forcing = finish(received[0], state, results[2], wet)
    return final_state.transpose(1, 0, 2), forcing.transpose(1, 0, 2)


def solution(mesh):
    return jax.shard_map(
        local,
        mesh=mesh,
        in_specs=(
            P(None, "lat", "sec"),
            P("lat", "sec"),
            P("lat", "sec"),
            P(),
            P(),
            P(),
            P(),
            P(),
            P(),
            P(),
        ),
        out_specs=(P(None, "lat", "sec"), P(None, "lat", "sec")),
        check_vma=False,
    )
```

```python
import functools

import jax
import jax.numpy as jnp
from jax import lax
from jax.experimental import pallas as pl
from jax.experimental.pallas import tpu as pltpu
from jax.sharding import PartitionSpec as P

LEVELS = 8
STEPS = 4
HALO = 8
TIME_STEP = 0.3
DRAG = 0.05
ROWS = 16
COLS = 256
EXT_ROWS = ROWS + 2 * HALO
WIDE = COLS + 128
SIDE = 64
MARGINS = tuple(HALO * (STEPS - step) for step in range(STEPS))
LAND_OFFSET = -(2.0**24)
F32 = jnp.float32
BF16 = jnp.bfloat16


def banded_kernel(*refs):
    weight_refs, bias_refs, band_refs, row_refs = refs[:4], refs[4:7], refs[7:11], refs[11:14]
    flat_ref, turned_ref = refs[14:]
    for layer in range(4):
        weight_ref, band_ref = weight_refs[layer], band_refs[layer]
        out_width = weight_ref.shape[1]
        in_width = weight_ref.shape[2] // 5
        in_pad = band_ref.shape[0] // 40
        wide = -(-5 * in_width // 128) * 128
        flat_ref[...] = jnp.zeros(flat_ref.shape, F32)
        for offset in range(5):
            flat_ref[0:out_width, 0 : 5 * in_width] = weight_ref[offset].astype(F32)
            turned_ref[offset, 0:wide, :] = jnp.transpose(flat_ref[:, 0:wide])
        extra = in_pad - in_width
        for half in range(2):
            for shift in range(5):
                for row in range(4):
                    parts = []
                    for out_row in range(4):
                        offset = 4 * half + row - out_row
                        if not 0 <= offset < 5:
                            parts.append(jnp.zeros((in_pad, out_width), F32))
                            continue
                        part = turned_ref[
                            offset, shift * in_width : (shift + 1) * in_width, 0:out_width
                        ]
                        if extra:
                            pad = jnp.zeros((extra, out_width), F32)
                            if layer == 0 and offset == 2 and shift == 2:
                                first = lax.broadcasted_iota(jnp.int32, pad.shape, 0) == 0
                                pad = jnp.where(first, LAND_OFFSET, 0.0)
                            part = jnp.concatenate([part, pad], axis=0)
                        parts.append(part)
                    if 4 * out_width < band_ref.shape[1]:
                        parts.append(jnp.zeros((in_pad, band_ref.shape[1] - 4 * out_width), F32))
                    base = ((half * 5 + shift) * 4 + row) * in_pad
                    band_ref[base : base + in_pad, :] = jnp.concatenate(parts, axis=1).astype(BF16)
    for bias_ref, row_ref in zip(bias_refs, row_refs):
        row_ref[...] = jnp.concatenate([bias_ref[...]] * 4, axis=1)


def banded(weights, biases):
    shapes = [(1280, 512), (5120, 256), (2560, 128), (1280, 128)]
    outs = [jax.ShapeDtypeStruct(shape, BF16) for shape in shapes]
    outs += [jax.ShapeDtypeStruct((1, width), F32) for width in (512, 256, 128)]
    return pl.pallas_call(
        banded_kernel,
        out_shape=outs,
        scratch_shapes=[pltpu.VMEM((128, 640), F32), pltpu.VMEM((5, 640, 128), F32)],
        name="banded",
    )(*weights, *[bias[None] for bias in biases])


def prepare_kernel(state_ref, land_ref, count_ref, own_ref, left_ref, right_ref):
    levels = land_ref[...] * count_ref[...]
    own_ref[:, 24:32, :] = jnp.zeros((ROWS, 8, COLS), F32)
    own_ref[:, 24, :] = levels.astype(F32)
    for channel in range(24):
        wet = jnp.where(levels > channel % LEVELS, 1.0, 0.0)
        own_ref[:, channel, :] = state_ref[channel] * wet
    flat = own_ref[...].reshape(ROWS * 32, COLS).astype(BF16)
    left_ref[...] = flat[:, 0:128]
    right_ref[...] = flat[:, COLS - 128 :]


def prepare(ocean_state, land_mask, layer_count):
    return pl.pallas_call(
        prepare_kernel,
        out_shape=[jax.ShapeDtypeStruct((ROWS, 32, COLS), F32)]
        + [jax.ShapeDtypeStruct((ROWS * 32, 128), BF16)] * 2,
        name="prepare",
    )(ocean_state, land_mask, layer_count)


def conv_rows(in_ref, weight_ref, group, count):
    lhs = jnp.concatenate([in_ref[group, 0:count, :], in_ref[group + 1, 0:count, :]], axis=1)
    return jnp.dot(lhs, weight_ref[...], preferred_element_type=F32)


def spread(value, work_ref, out_ref, group, width):
    span = value.shape[0]
    work_ref[0:span, 0:width] = value
    for shift in range(5):
        out_ref[group, :, shift * width : (shift + 1) * width] = work_ref[
            shift : shift + span, 0:width
        ].astype(BF16)


def conv_layer(in_ref, weight_ref, bias_ref, sea_ref, work_ref, out_ref, layer, groups):
    width = weight_ref.shape[1]

    def body(group, carry):
        half = 0.5 * (conv_rows(in_ref, weight_ref, group, in_ref.shape[1]) + bias_ref[...])
        value = half + half * jnp.tanh(half)
        if layer:
            row_of = lax.broadcasted_iota(jnp.int32, (128, width), 0)
            lane_of = lax.broadcasted_iota(jnp.int32, (128, width), 1)
            wanted = 4 * group + 2 * (layer + 1) + lane_of // (width // 4)
            pick = jnp.where(row_of == wanted, 1.0, 0.0).astype(BF16)
            value = value * jnp.dot(sea_ref[layer - 1], pick, preferred_element_type=F32)
        spread(value, work_ref, out_ref, group, width)
        return carry

    lax.fori_loop(0, groups, body, 0)


def device_means(received):
    total = jnp.sum(received, axis=0, keepdims=True)
    column = jnp.transpose(jnp.broadcast_to(total, (128, 128)))
    counts = jnp.maximum(column[16:24], 1.0)
    return column[0:8] / counts, column[8:16] / counts


def step_kernel(*refs, step):
    first, last = step == 0, step == STEPS - 1
    margin = MARGINS[step]
    span = COLS + 2 * margin
    refs = list(refs)
    start_ref = refs.pop(0)
    own_ref, top_ref, bottom_ref = refs[:3]
    refs = refs[3:]
    if first:
        left_ref, right_ref = refs[:2]
        refs = refs[2:]
    else:
        recv_ref, wet_ref, sea_turned_ref = refs[:3]
        refs = refs[3:]
    w1_ref, w2_ref, w3_ref, w4_ref, b1_ref, b2_ref, b3_ref, new_ref, pay_ref = refs[:9]
    refs = refs[9:]
    if first:
        wet_ref, sea_turned_ref = refs[:2]
        refs = refs[2:]
    if last:
        raw_out_ref = refs.pop(0)
    else:
        send_up_ref, send_down_ref = refs[:2]
        refs = refs[2:]
    state_ref, a0_ref, a1_ref, a2_ref, a3_ref, work_ref, raw_ref, sea_ref = refs

    if first:
        lane = lax.broadcasted_iota(jnp.int32, (ROWS * 32, 128), 1)
        sides = jnp.where(lane < SIDE, right_ref[...].astype(F32), left_ref[...].astype(F32))
        state_ref[HALO : HALO + ROWS, :, 0:COLS] = own_ref[...]
        state_ref[HALO : HALO + ROWS, :, COLS:WIDE] = sides.reshape(ROWS, 32, 128)
        state_ref[0:HALO] = top_ref[...].astype(F32).reshape(HALO, 32, WIDE)
        state_ref[HALO + ROWS :] = bottom_ref[...].astype(F32).reshape(HALO, 32, WIDE)
        levels = jnp.broadcast_to(state_ref[:, 24:25, :], (EXT_ROWS, 8, WIDE))
        level_of = lax.broadcasted_iota(jnp.int32, levels.shape, 1).astype(F32)
        wet_ref[...] = jnp.where(level_of < levels, 1.0, 0.0)
        by_row = jnp.where(state_ref[:, 24, :] > 0.0, 1.0, 0.0)
        turned = jnp.transpose(
            jnp.concatenate([by_row, jnp.zeros((128 - EXT_ROWS, WIDE), F32)], axis=0)
        )
        sea_turned_ref[0:SIDE, :] = turned[WIDE - SIDE :]
        sea_turned_ref[SIDE:WIDE, :] = turned[0 : WIDE - SIDE]
        sea_turned_ref[WIDE:, :] = jnp.zeros((8, 128), F32)
    else:
        state_ref[HALO : HALO + ROWS, 0:24, :] = own_ref[...]
        state_ref[0:HALO, 0:24, :] = top_ref[...].astype(F32).reshape(HALO, 24, WIDE)
        state_ref[HALO + ROWS :, 0:24, :] = bottom_ref[...].astype(F32).reshape(HALO, 24, WIDE)
        zonal_mean, merid_mean = device_means(recv_ref[...])
        for base, mean in ((0, zonal_mean), (8, merid_mean)):
            scaled = jnp.concatenate([TIME_STEP * mean] * 3, axis=1)
            state_ref[:, base : base + 8, :] = (
                state_ref[:, base : base + 8, :] - scaled[None] * wet_ref[...]
            )
    first_channel = lax.broadcasted_iota(jnp.int32, (EXT_ROWS, 8, WIDE), 1) == 0
    state_ref[:, 24:32, :] = jnp.where(first_channel, 1.0 - wet_ref[...], 0.0)
    for layer in (1, 2):
        begin = SIDE - margin + 2 * (layer + 1)
        sea_ref[layer - 1] = sea_turned_ref[begin : begin + span, :].astype(BF16)

    work_ref[span:, :] = jnp.zeros((8, 512), F32)
    for group in range(8):
        flat = state_ref[4 * group : 4 * group + 4].reshape(128, WIDE)
        turned = jnp.transpose(flat)
        spread(
            jnp.concatenate([turned[WIDE - margin :], turned[0 : COLS + margin]], axis=0),
            work_ref,
            a0_ref,
            group,
            128,
        )
    conv_layer(a0_ref, w1_ref, b1_ref, sea_ref, work_ref, a1_ref, 0, 7)
    conv_layer(a1_ref, w2_ref, b2_ref, sea_ref, work_ref, a2_ref, 1, 6)
    conv_layer(a2_ref, w3_ref, b3_ref, sea_ref, work_ref, a3_ref, 2, 5)
    left = margin - HALO
    for group in range(4):
        found = conv_rows(a3_ref, w4_ref, group, COLS + 2 * left)
        around = [found[left:], jnp.zeros((WIDE - COLS - 2 * left, 128), F32)]
        if left:
            around.append(found[:left])
        turned = jnp.transpose(jnp.concatenate(around, axis=0))
        raw_ref[4 * group : 4 * group + 4] = turned[0:64].reshape(4, 16, WIDE)

    def shifted_difference(field):
        return (pltpu.roll(field, WIDE - 1, 2) - pltpu.roll(field, 1, 2)) * 0.5

    rows = ROWS + 2
    low = HALO - 1
    zonal = state_ref[low : low + rows, 0:8, :]
    merid_above = state_ref[low + 1 : low + 1 + rows, 8:16, :]
    merid_below = state_ref[low - 1 : low - 1 + rows, 8:16, :]
    divergence = shifted_difference(zonal) + (merid_above - merid_below) * 0.5
    thickness = state_ref[low : low + rows, 16:24, :]
    h_new = (thickness - TIME_STEP * divergence) * wet_ref[low : low + rows]
    level = lax.broadcasted_iota(jnp.int32, (1, 8, 1), 1)
    pressure = None
    for other in range(LEVELS):
        weight = 0.5 + 0.1 * jnp.minimum(level, other).astype(F32)
        term = weight * h_new[:, other : other + 1, :]
        pressure = term if pressure is None else pressure + term
    grad_x = shifted_difference(pressure[1:-1])
    grad_y = (pressure[2:] - pressure[:-2]) * 0.5
    wet = wet_ref[HALO : HALO + ROWS]
    zonal_mid = state_ref[HALO : HALO + ROWS, 0:8, :]
    merid_mid = state_ref[HALO : HALO + ROWS, 8:16, :]
    global_row = start_ref[0] + lax.broadcasted_iota(jnp.int32, (ROWS, 8, WIDE), 0)
    coriolis = 0.3 + 0.5 * global_row.astype(F32) / 512.0
    raw_zonal = raw_ref[:, 0:8, :]
    raw_merid = raw_ref[:, 8:16, :]
    zonal_new = (
        zonal_mid + TIME_STEP * (-grad_x + coriolis * merid_mid - DRAG * zonal_mid + raw_zonal)
    ) * wet
    merid_new = (
        merid_mid + TIME_STEP * (-grad_y - coriolis * zonal_mid - DRAG * merid_mid + raw_merid)
    ) * wet
    new_ref[:, 0:8, :] = zonal_new
    new_ref[:, 8:16, :] = merid_new
    new_ref[:, 16:24, :] = h_new[1:-1]
    if last:
        raw_out_ref[...] = raw_ref[...]
    else:
        flat = new_ref[...].reshape(ROWS * 24, WIDE).astype(BF16)
        send_down_ref[...] = flat[0 : HALO * 24]
        send_up_ref[...] = flat[(ROWS - HALO) * 24 :]

    def lanes_of(field):
        by_column = jnp.sum(field, axis=0)
        return by_column[:, 0:128] + by_column[:, 128:256]

    columns = jnp.concatenate(
        [
            lanes_of(raw_zonal * wet),
            lanes_of(raw_merid * wet),
            lanes_of(wet),
            jnp.zeros((104, 128), F32),
        ],
        axis=0,
    )
    row = jnp.sum(jnp.transpose(columns), axis=0, keepdims=True)
    pay_ref[...] = jnp.broadcast_to(row, (128, 128))


def ocean_network_step(step, args):
    first, last = step == 0, step == STEPS - 1
    span = COLS + 2 * MARGINS[step]
    outs = [
        jax.ShapeDtypeStruct((ROWS, 24, WIDE), F32),
        jax.ShapeDtypeStruct((128, 128), F32),
    ]
    if first:
        outs.append(jax.ShapeDtypeStruct((EXT_ROWS, LEVELS, WIDE), F32))
        outs.append(jax.ShapeDtypeStruct((WIDE + 8, 128), F32))
    if last:
        outs.append(jax.ShapeDtypeStruct((ROWS, 16, WIDE), F32))
    else:
        outs += [jax.ShapeDtypeStruct((HALO * 24, WIDE), BF16)] * 2
    vmem = pl.BlockSpec(memory_space=pltpu.VMEM)
    return pl.pallas_call(
        functools.partial(step_kernel, step=step),
        out_shape=outs,
        in_specs=[pl.BlockSpec(memory_space=pltpu.SMEM)] + [vmem] * (len(args) - 1),
        out_specs=[vmem] * len(outs),
        scratch_shapes=[
            pltpu.VMEM((EXT_ROWS, 32, WIDE), F32),
            pltpu.VMEM((8, span, 5 * 128), BF16),
            pltpu.VMEM((7, span, 5 * 512), BF16),
            pltpu.VMEM((6, span, 5 * 256), BF16),
            pltpu.VMEM((5, span, 5 * 128), BF16),
            pltpu.VMEM((span + 8, 512), F32),
            pltpu.VMEM((ROWS, 16, WIDE), F32),
            pltpu.VMEM((2, span, 128), BF16),
        ],
        name=f"step_{step}",
    )(*args)


def finish_kernel(recv_ref, state_ref, raw_ref, wet_ref, final_ref, forcing_ref, work_ref):
    zonal_mean, merid_mean = device_means(recv_ref[...])
    wet = wet_ref[HALO : HALO + ROWS, :, 0:COLS]
    zonal_mean = jnp.concatenate([zonal_mean] * 2, axis=1)[None]
    merid_mean = jnp.concatenate([merid_mean] * 2, axis=1)[None]
    work_ref[:, 0:8, :] = (raw_ref[:, 0:8, 0:COLS] - zonal_mean) * wet
    work_ref[:, 8:16, :] = (raw_ref[:, 8:16, 0:COLS] - merid_mean) * wet
    for channel in range(16):
        forcing_ref[channel] = work_ref[:, channel, :]
    work_ref[:, 0:8, :] = state_ref[:, 0:8, 0:COLS] - TIME_STEP * zonal_mean * wet
    work_ref[:, 8:16, :] = state_ref[:, 8:16, 0:COLS] - TIME_STEP * merid_mean * wet
    for channel in range(16):
        final_ref[channel] = work_ref[:, channel, :]
    for channel in range(16, 24):
        final_ref[channel] = state_ref[:, channel, 0:COLS]


def finish(received, state, raw, wet):
    return pl.pallas_call(
        finish_kernel,
        out_shape=[
            jax.ShapeDtypeStruct((24, ROWS, COLS), F32),
            jax.ShapeDtypeStruct((16, ROWS, COLS), F32),
        ],
        scratch_shapes=[pltpu.VMEM((ROWS, 16, COLS), F32)],
        name="finish",
    )(received, state, raw, wet)


def both_ways(axis, up, down):
    count = lax.axis_size(axis)
    forward = [(i, i + 1) for i in range(count - 1)]
    backward = [(target, source) for source, target in forward]
    return lax.ppermute(up, axis, forward), lax.ppermute(down, axis, backward)


def local(
    ocean_state,
    land_mask,
    layer_count,
    conv1_weight,
    conv1_bias,
    conv2_weight,
    conv2_bias,
    conv3_weight,
    conv3_bias,
    conv4_weight,
):
    state, send_left, send_right = prepare(ocean_state, land_mask, layer_count)
    left, right = both_ways("sec", send_right, send_left)
    weights = banded(
        [conv1_weight, conv2_weight, conv3_weight, conv4_weight],
        [conv1_bias, conv2_bias, conv3_bias],
    )
    lane = lax.broadcasted_iota(jnp.int32, left.shape, 1)
    sides = jnp.where(lane < SIDE, right, left)
    whole = jnp.concatenate([send_left, send_right, sides], axis=1)
    halos = both_ways("lat", whole[HALO * 32 :], whole[: HALO * 32])

    start = (lax.axis_index("lat") * ROWS).astype(jnp.int32)[None]
    extras = [left, right]
    for step in range(STEPS):
        results = ocean_network_step(step, [start, state, *halos, *extras, *weights])
        state = results[0]
        if step == 0:
            wet, sea = results[2:4]
        if step < STEPS - 1:
            halos = both_ways("lat", results[-2], results[-1])
        received = lax.all_to_all(results[1], ("sec", "lat"), 0, 0)
        extras = [received, wet, sea]
    return finish(received, state, results[2], wet)


def solution(mesh):
    return jax.shard_map(
        local,
        mesh=mesh,
        in_specs=(
            P(None, "lat", "sec"),
            P("lat", "sec"),
            P("lat", "sec"),
            P(),
            P(),
            P(),
            P(),
            P(),
            P(),
            P(),
        ),
        out_specs=(P(None, "lat", "sec"), P(None, "lat", "sec")),
        check_vma=False,
    )
```

```python
import functools

import jax
import jax.numpy as jnp
from jax import lax
from jax.experimental import pallas as pl
from jax.experimental.pallas import tpu as pltpu
from jax.sharding import PartitionSpec as P

LEVELS = 8
STEPS = 4
HALO = 8
TIME_STEP = 0.3
DRAG = 0.05
ROWS = 16
COLS = 256
EXT_ROWS = ROWS + 2 * HALO
WIDE = COLS + 128
SIDE = 64
MARGINS = tuple(HALO * (STEPS - step) for step in range(STEPS))
LAND_OFFSET = -(2.0**24)
PADDED = (32, 128, 64, 32)
F32 = jnp.float32
BF16 = jnp.bfloat16


def banded_kernel(*refs):
    weight_refs, bias_refs, band_refs, row_refs = refs[:4], refs[4:7], refs[7:11], refs[11:14]
    flat_ref, turned_ref = refs[14:]
    for layer in range(4):
        weight_ref, band_ref = weight_refs[layer], band_refs[layer]
        out_width = weight_ref.shape[1]
        in_width = weight_ref.shape[2] // 5
        in_pad = PADDED[layer]
        groups = band_ref.shape[0] // (20 * in_pad)
        out_rows = band_ref.shape[1] // out_width
        wide = -(-5 * in_width // 128) * 128
        flat_ref[...] = jnp.zeros(flat_ref.shape, F32)
        for offset in range(5):
            flat_ref[0:out_width, 0 : 5 * in_width] = weight_ref[offset].astype(F32)
            turned_ref[offset, 0:wide, :] = jnp.transpose(flat_ref[:, 0:wide])
        extra = in_pad - in_width
        for group in range(groups):
            for shift in range(5):
                for row in range(4):
                    parts = []
                    for out_row in range(out_rows):
                        offset = 4 * group + row - out_row
                        if not 0 <= offset < 5:
                            parts.append(jnp.zeros((in_pad, out_width), F32))
                            continue
                        part = turned_ref[
                            offset, shift * in_width : (shift + 1) * in_width, 0:out_width
                        ]
                        if extra:
                            pad = jnp.zeros((extra, out_width), F32)
                            if layer == 0 and offset == 2 and shift == 2:
                                first = lax.broadcasted_iota(jnp.int32, pad.shape, 0) == 0
                                pad = jnp.where(first, LAND_OFFSET, 0.0)
                            part = jnp.concatenate([part, pad], axis=0)
                        parts.append(part)
                    base = ((group * 5 + shift) * 4 + row) * in_pad
                    band_ref[base : base + in_pad, :] = jnp.concatenate(parts, axis=1).astype(BF16)
    for bias_ref, row_ref in zip(bias_refs, row_refs):
        row_ref[...] = jnp.concatenate([bias_ref[...]] * 4, axis=1)


def banded(weights, biases):
    shapes = [(1280, 512), (5120, 256), (2560, 128), (3200, 256)]
    outs = [jax.ShapeDtypeStruct(shape, BF16) for shape in shapes]
    outs += [jax.ShapeDtypeStruct((1, width), F32) for width in (512, 256, 128)]
    return pl.pallas_call(
        banded_kernel,
        out_shape=outs,
        scratch_shapes=[pltpu.VMEM((128, 640), F32), pltpu.VMEM((5, 640, 128), F32)],
        name="banded",
    )(*weights, *[bias[None] for bias in biases])


def prepare_kernel(state_ref, land_ref, count_ref, own_ref, left_ref, right_ref):
    levels = land_ref[...] * count_ref[...]
    own_ref[:, 24:32, :] = jnp.zeros((ROWS, 8, COLS), F32)
    own_ref[:, 24, :] = levels.astype(F32)
    for channel in range(24):
        wet = jnp.where(levels > channel % LEVELS, 1.0, 0.0)
        own_ref[:, channel, :] = state_ref[channel] * wet
    flat = own_ref[...].reshape(ROWS * 32, COLS).astype(BF16)
    left_ref[...] = flat[:, 0:128]
    right_ref[...] = flat[:, COLS - 128 :]


def prepare(ocean_state, land_mask, layer_count):
    return pl.pallas_call(
        prepare_kernel,
        out_shape=[jax.ShapeDtypeStruct((ROWS, 32, COLS), F32)]
        + [jax.ShapeDtypeStruct((ROWS * 32, 128), BF16)] * 2,
        name="prepare",
    )(ocean_state, land_mask, layer_count)


def spread(value, work_ref, out_ref, group, zero):
    span, width = value.shape
    out_ref[group, :, 0:width] = value.astype(BF16)
    for tile in range(width // 128):
        work_ref[tile, 0:span, :] = value[:, 128 * tile : 128 * tile + 128]
    for shift in range(1, 5):
        for tile in range(width // 128):
            base = shift * width + 128 * tile
            out_ref[group, :, base : base + 128] = work_ref[
                tile, pl.ds(zero + shift, span), :
            ].astype(BF16)


def conv_layer(refs, raw_ref, sea_ref, work_ref, zero, layer, groups):
    in_ref, weight_ref, bias_ref, out_ref = refs
    width = weight_ref.shape[1]

    def activate(group):
        half = 0.5 * (raw_ref[:, 0:width] + bias_ref[...])
        value = half + half * jnp.tanh(half)
        if layer:
            row_of = lax.broadcasted_iota(jnp.int32, (128, width), 0)
            lane_of = lax.broadcasted_iota(jnp.int32, (128, width), 1)
            wanted = 4 * group + 2 * (layer + 1) + lane_of // (width // 4)
            pick = jnp.where(row_of == wanted, 1.0, 0.0).astype(BF16)
            value = value * jnp.dot(sea_ref[layer - 1], pick, preferred_element_type=F32)
        spread(value, work_ref, out_ref, group, zero)

    def body(group, carry):
        activate(jnp.maximum(group - 1, 0))
        lhs = jnp.concatenate([in_ref[group], in_ref[group + 1]], axis=1)
        raw_ref[:, 0:width] = jnp.dot(lhs, weight_ref[...], preferred_element_type=F32)
        return carry

    lax.fori_loop(0, groups, body, 0)
    activate(groups - 1)


def device_means(received):
    total = jnp.sum(received, axis=0, keepdims=True)
    column = jnp.transpose(jnp.broadcast_to(total, (128, 128)))
    counts = jnp.maximum(column[16:24], 1.0)
    return column[0:8] / counts, column[8:16] / counts


def step_kernel(*refs, step):
    first, last = step == 0, step == STEPS - 1
    margin = MARGINS[step]
    span = COLS + 2 * margin
    refs = list(refs)
    start_ref = refs.pop(0)
    own_ref, top_ref, bottom_ref = refs[:3]
    refs = refs[3:]
    if first:
        left_ref, right_ref = refs[:2]
        refs = refs[2:]
    else:
        recv_ref, wet_ref, sea_turned_ref = refs[:3]
        refs = refs[3:]
    w1_ref, w2_ref, w3_ref, w4_ref, b1_ref, b2_ref, b3_ref, new_ref, pay_ref = refs[:9]
    refs = refs[9:]
    if first:
        wet_ref, sea_turned_ref = refs[:2]
        refs = refs[2:]
    if last:
        raw_out_ref = refs.pop(0)
    else:
        send_up_ref, send_down_ref = refs[:2]
        refs = refs[2:]
    state_ref, a0_ref, a1_ref, a2_ref, a3_ref, work_ref, raw_ref, sea_ref, sum_ref = refs
    zero = start_ref[1]

    if first:
        lane = lax.broadcasted_iota(jnp.int32, (ROWS * 32, 128), 1)
        sides = jnp.where(lane < SIDE, right_ref[...].astype(F32), left_ref[...].astype(F32))
        state_ref[HALO : HALO + ROWS, :, 0:COLS] = own_ref[...]
        state_ref[HALO : HALO + ROWS, :, COLS:WIDE] = sides.reshape(ROWS, 32, 128)
        state_ref[0:HALO] = top_ref[...].astype(F32).reshape(HALO, 32, WIDE)
        state_ref[HALO + ROWS :] = bottom_ref[...].astype(F32).reshape(HALO, 32, WIDE)
        levels = jnp.broadcast_to(state_ref[:, 24:25, :], (EXT_ROWS, 8, WIDE))
        level_of = lax.broadcasted_iota(jnp.int32, levels.shape, 1).astype(F32)
        wet_ref[...] = jnp.where(level_of < levels, 1.0, 0.0)
        by_row = jnp.where(state_ref[:, 24, :] > 0.0, 1.0, 0.0)
        turned = jnp.transpose(
            jnp.concatenate([by_row, jnp.zeros((128 - EXT_ROWS, WIDE), F32)], axis=0)
        )
        sea_turned_ref[0:SIDE, :] = turned[WIDE - SIDE :]
        sea_turned_ref[SIDE:WIDE, :] = turned[0 : WIDE - SIDE]
        sea_turned_ref[WIDE:, :] = jnp.zeros((8, 128), F32)
    else:
        state_ref[HALO : HALO + ROWS, 0:24, :] = own_ref[...]
        state_ref[0:HALO, 0:24, :] = top_ref[...].astype(F32).reshape(HALO, 24, WIDE)
        state_ref[HALO + ROWS :, 0:24, :] = bottom_ref[...].astype(F32).reshape(HALO, 24, WIDE)
        zonal_mean, merid_mean = device_means(recv_ref[...])
        for base, mean in ((0, zonal_mean), (8, merid_mean)):
            scaled = jnp.concatenate([TIME_STEP * mean] * 3, axis=1)
            state_ref[:, base : base + 8, :] = (
                state_ref[:, base : base + 8, :] - scaled[None] * wet_ref[...]
            )
    first_channel = lax.broadcasted_iota(jnp.int32, (EXT_ROWS, 8, WIDE), 1) == 0
    state_ref[:, 24:32, :] = jnp.where(first_channel, 1.0 - wet_ref[...], 0.0)
    for layer in (1, 2):
        begin = SIDE - margin + 2 * (layer + 1)
        sea_ref[layer - 1] = sea_turned_ref[begin : begin + span, :].astype(BF16)

    work_ref[:, span:, :] = jnp.zeros((4, 8, 128), F32)
    for group in range(8):
        flat = state_ref[4 * group : 4 * group + 4].reshape(128, WIDE)
        turned = jnp.transpose(flat)
        around = jnp.concatenate([turned[WIDE - margin :], turned[0 : COLS + margin]], axis=0)
        spread(around, work_ref, a0_ref, group, zero)
    for layer, refs in enumerate(
        (
            (a0_ref, w1_ref, b1_ref, a1_ref),
            (a1_ref, w2_ref, b2_ref, a2_ref),
            (a2_ref, w3_ref, b3_ref, a3_ref),
        )
    ):
        conv_layer(refs, sum_ref, sea_ref, work_ref, zero, layer, 7 - layer)
    left = margin - HALO
    count = COLS + 2 * left
    lhs = jnp.concatenate([a3_ref[group, 0:count, :] for group in range(5)], axis=1)
    found = jnp.dot(lhs, w4_ref[...], preferred_element_type=F32)
    around = [found[left:], jnp.zeros((WIDE - count, 256), F32)]
    if left:
        around.append(found[:left])
    raw_ref[...] = jnp.transpose(jnp.concatenate(around, axis=0)).reshape(ROWS, 16, WIDE)

    def shifted_difference(field):
        return (pltpu.roll(field, WIDE - 1, 2) - pltpu.roll(field, 1, 2)) * 0.5

    rows = ROWS + 2
    low = HALO - 1
    zonal = state_ref[low : low + rows, 0:8, :]
    merid_above = state_ref[low + 1 : low + 1 + rows, 8:16, :]
    merid_below = state_ref[low - 1 : low - 1 + rows, 8:16, :]
    divergence = shifted_difference(zonal) + (merid_above - merid_below) * 0.5
    thickness = state_ref[low : low + rows, 16:24, :]
    h_new = (thickness - TIME_STEP * divergence) * wet_ref[low : low + rows]
    level = lax.broadcasted_iota(jnp.int32, (1, 8, 1), 1)
    pressure = None
    for other in range(LEVELS):
        weight = 0.5 + 0.1 * jnp.minimum(level, other).astype(F32)
        term = weight * h_new[:, other : other + 1, :]
        pressure = term if pressure is None else pressure + term
    grad_x = shifted_difference(pressure[1:-1])
    grad_y = (pressure[2:] - pressure[:-2]) * 0.5
    wet = wet_ref[HALO : HALO + ROWS]
    zonal_mid = state_ref[HALO : HALO + ROWS, 0:8, :]
    merid_mid = state_ref[HALO : HALO + ROWS, 8:16, :]
    global_row = start_ref[0] + lax.broadcasted_iota(jnp.int32, (ROWS, 8, WIDE), 0)
    coriolis = 0.3 + 0.5 * global_row.astype(F32) / 512.0
    raw_zonal = raw_ref[:, 0:8, :]
    raw_merid = raw_ref[:, 8:16, :]
    zonal_new = (
        zonal_mid + TIME_STEP * (-grad_x + coriolis * merid_mid - DRAG * zonal_mid + raw_zonal)
    ) * wet
    merid_new = (
        merid_mid + TIME_STEP * (-grad_y - coriolis * zonal_mid - DRAG * merid_mid + raw_merid)
    ) * wet
    new_ref[:, 0:8, :] = zonal_new
    new_ref[:, 8:16, :] = merid_new
    new_ref[:, 16:24, :] = h_new[1:-1]
    if last:
        raw_out_ref[...] = raw_ref[...]
    else:
        flat = new_ref[...].reshape(ROWS * 24, WIDE).astype(BF16)
        send_down_ref[...] = flat[0 : HALO * 24]
        send_up_ref[...] = flat[(ROWS - HALO) * 24 :]

    def lanes_of(field):
        by_column = jnp.sum(field, axis=0)
        return by_column[:, 0:128] + by_column[:, 128:256]

    columns = jnp.concatenate(
        [
            lanes_of(raw_zonal * wet),
            lanes_of(raw_merid * wet),
            lanes_of(wet),
            jnp.zeros((104, 128), F32),
        ],
        axis=0,
    )
    row = jnp.sum(jnp.transpose(columns), axis=0, keepdims=True)
    pay_ref[...] = jnp.broadcast_to(row, (128, 128))


def ocean_network_step(step, args):
    first, last = step == 0, step == STEPS - 1
    span = COLS + 2 * MARGINS[step]
    outs = [
        jax.ShapeDtypeStruct((ROWS, 24, WIDE), F32),
        jax.ShapeDtypeStruct((128, 128), F32),
    ]
    if first:
        outs.append(jax.ShapeDtypeStruct((EXT_ROWS, LEVELS, WIDE), F32))
        outs.append(jax.ShapeDtypeStruct((WIDE + 8, 128), F32))
    if last:
        outs.append(jax.ShapeDtypeStruct((ROWS, 16, WIDE), F32))
    else:
        outs += [jax.ShapeDtypeStruct((HALO * 24, WIDE), BF16)] * 2
    vmem = pl.BlockSpec(memory_space=pltpu.VMEM)
    return pl.pallas_call(
        functools.partial(step_kernel, step=step),
        out_shape=outs,
        in_specs=[pl.BlockSpec(memory_space=pltpu.SMEM)] + [vmem] * (len(args) - 1),
        out_specs=[vmem] * len(outs),
        scratch_shapes=[
            pltpu.VMEM((EXT_ROWS, 32, WIDE), F32),
            pltpu.VMEM((8, span, 5 * 128), BF16),
            pltpu.VMEM((7, span, 5 * 512), BF16),
            pltpu.VMEM((6, span, 5 * 256), BF16),
            pltpu.VMEM((5, span, 5 * 128), BF16),
            pltpu.VMEM((4, span + 8, 128), F32),
            pltpu.VMEM((ROWS, 16, WIDE), F32),
            pltpu.VMEM((2, span, 128), BF16),
            pltpu.VMEM((span, 512), F32),
        ],
        name=f"step_{step}",
    )(*args)


def finish_kernel(recv_ref, state_ref, raw_ref, wet_ref, final_ref, forcing_ref, work_ref):
    zonal_mean, merid_mean = device_means(recv_ref[...])
    wet = wet_ref[HALO : HALO + ROWS, :, 0:COLS]
    zonal_mean = jnp.concatenate([zonal_mean] * 2, axis=1)[None]
    merid_mean = jnp.concatenate([merid_mean] * 2, axis=1)[None]
    work_ref[:, 0:8, :] = (raw_ref[:, 0:8, 0:COLS] - zonal_mean) * wet
    work_ref[:, 8:16, :] = (raw_ref[:, 8:16, 0:COLS] - merid_mean) * wet
    for channel in range(16):
        forcing_ref[channel] = work_ref[:, channel, :]
    work_ref[:, 0:8, :] = state_ref[:, 0:8, 0:COLS] - TIME_STEP * zonal_mean * wet
    work_ref[:, 8:16, :] = state_ref[:, 8:16, 0:COLS] - TIME_STEP * merid_mean * wet
    for channel in range(16):
        final_ref[channel] = work_ref[:, channel, :]
    for channel in range(16, 24):
        final_ref[channel] = state_ref[:, channel, 0:COLS]


def finish(received, state, raw, wet):
    return pl.pallas_call(
        finish_kernel,
        out_shape=[
            jax.ShapeDtypeStruct((24, ROWS, COLS), F32),
            jax.ShapeDtypeStruct((16, ROWS, COLS), F32),
        ],
        scratch_shapes=[pltpu.VMEM((ROWS, 16, COLS), F32)],
        name="finish",
    )(received, state, raw, wet)


def both_ways(axis, up, down):
    count = lax.axis_size(axis)
    forward = [(i, i + 1) for i in range(count - 1)]
    backward = [(target, source) for source, target in forward]
    return lax.ppermute(up, axis, forward), lax.ppermute(down, axis, backward)


def local(
    ocean_state,
    land_mask,
    layer_count,
    conv1_weight,
    conv1_bias,
    conv2_weight,
    conv2_bias,
    conv3_weight,
    conv3_bias,
    conv4_weight,
):
    state, send_left, send_right = prepare(ocean_state, land_mask, layer_count)
    left, right = both_ways("sec", send_right, send_left)
    weights = banded(
        [conv1_weight, conv2_weight, conv3_weight, conv4_weight],
        [conv1_bias, conv2_bias, conv3_bias],
    )
    lane = lax.broadcasted_iota(jnp.int32, left.shape, 1)
    sides = jnp.where(lane < SIDE, right, left)
    whole = jnp.concatenate([send_left, send_right, sides], axis=1)
    halos = both_ways("lat", whole[HALO * 32 :], whole[: HALO * 32])

    start = (lax.axis_index("lat") * ROWS).astype(jnp.int32)
    start = jnp.stack([start, jnp.zeros((), jnp.int32)])
    extras = [left, right]
    for step in range(STEPS):
        results = ocean_network_step(step, [start, state, *halos, *extras, *weights])
        state = results[0]
        if step == 0:
            wet, sea = results[2:4]
        if step < STEPS - 1:
            halos = both_ways("lat", results[-2], results[-1])
        received = lax.all_to_all(results[1], ("sec", "lat"), 0, 0)
        extras = [received, wet, sea]
    return finish(received, state, results[2], wet)


def solution(mesh):
    return jax.shard_map(
        local,
        mesh=mesh,
        in_specs=(
            P(None, "lat", "sec"),
            P("lat", "sec"),
            P("lat", "sec"),
            P(),
            P(),
            P(),
            P(),
            P(),
            P(),
            P(),
        ),
        out_specs=(P(None, "lat", "sec"), P(None, "lat", "sec")),
        check_vma=False,
    )
```

```python
import functools

import jax
import jax.numpy as jnp
from jax import lax
from jax.experimental import pallas as pl
from jax.experimental.pallas import tpu as pltpu
from jax.sharding import PartitionSpec as P

LEVELS = 8
STEPS = 4
HALO = 8
TIME_STEP = 0.3
DRAG = 0.05
ROWS = 16
COLS = 256
EXT_ROWS = ROWS + 2 * HALO
WIDE = COLS + 128
SIDE = 64
MARGINS = tuple(HALO * (STEPS - step) for step in range(STEPS))
LAND_OFFSET = -(2.0**24)
PADDED = (32, 128, 64, 32)
F32 = jnp.float32
BF16 = jnp.bfloat16


def banded_kernel(*refs):
    weight_refs, bias_refs, band_refs, row_refs = refs[:4], refs[4:7], refs[7:11], refs[11:14]
    flat_ref, turned_ref = refs[14:]
    for layer in range(4):
        weight_ref, band_ref = weight_refs[layer], band_refs[layer]
        out_width = weight_ref.shape[1]
        in_width = weight_ref.shape[2] // 5
        in_pad = PADDED[layer]
        groups = band_ref.shape[0] // (20 * in_pad)
        out_rows = band_ref.shape[1] // out_width
        wide = -(-5 * in_width // 128) * 128
        flat_ref[...] = jnp.zeros(flat_ref.shape, F32)
        for offset in range(5):
            flat_ref[0:out_width, 0 : 5 * in_width] = weight_ref[offset].astype(F32)
            turned_ref[offset, 0:wide, :] = jnp.transpose(flat_ref[:, 0:wide])
        extra = in_pad - in_width
        for group in range(groups):
            for shift in range(5):
                for row in range(4):
                    parts = []
                    for out_row in range(out_rows):
                        offset = 4 * group + row - out_row
                        if not 0 <= offset < 5:
                            parts.append(jnp.zeros((in_pad, out_width), F32))
                            continue
                        part = turned_ref[
                            offset, shift * in_width : (shift + 1) * in_width, 0:out_width
                        ]
                        if extra:
                            pad = jnp.zeros((extra, out_width), F32)
                            if layer == 0 and offset == 2 and shift == 2:
                                first = lax.broadcasted_iota(jnp.int32, pad.shape, 0) == 0
                                pad = jnp.where(first, LAND_OFFSET, 0.0)
                            part = jnp.concatenate([part, pad], axis=0)
                        parts.append(part)
                    base = ((group * 5 + shift) * 4 + row) * in_pad
                    band_ref[base : base + in_pad, :] = jnp.concatenate(parts, axis=1).astype(BF16)
    for bias_ref, row_ref in zip(bias_refs, row_refs):
        row_ref[...] = jnp.concatenate([bias_ref[...]] * 4, axis=1)


def banded(weights, biases):
    shapes = [(1280, 512), (5120, 256), (2560, 128), (3200, 256)]
    outs = [jax.ShapeDtypeStruct(shape, BF16) for shape in shapes]
    outs += [jax.ShapeDtypeStruct((1, width), F32) for width in (512, 256, 128)]
    return pl.pallas_call(
        banded_kernel,
        out_shape=outs,
        scratch_shapes=[pltpu.VMEM((128, 640), F32), pltpu.VMEM((5, 640, 128), F32)],
        compiler_params=pltpu.CompilerParams(vmem_limit_bytes=24 * 2**20),
        name="banded",
    )(*weights, *[bias[None] for bias in biases])


def prepare_kernel(state_ref, land_ref, count_ref, own_ref, left_ref, right_ref):
    levels = land_ref[...] * count_ref[...]
    own_ref[:, 24:32, :] = jnp.zeros((ROWS, 8, COLS), F32)
    own_ref[:, 24, :] = levels.astype(F32)
    for channel in range(24):
        wet = jnp.where(levels > channel % LEVELS, 1.0, 0.0)
        own_ref[:, channel, :] = state_ref[channel] * wet
    flat = own_ref[...].reshape(ROWS * 32, COLS).astype(BF16)
    left_ref[...] = flat[:, 0:128]
    right_ref[...] = flat[:, COLS - 128 :]


def prepare(ocean_state, land_mask, layer_count):
    return pl.pallas_call(
        prepare_kernel,
        out_shape=[jax.ShapeDtypeStruct((ROWS, 32, COLS), F32)]
        + [jax.ShapeDtypeStruct((ROWS * 32, 128), BF16)] * 2,
        compiler_params=pltpu.CompilerParams(vmem_limit_bytes=24 * 2**20),
        name="prepare",
    )(ocean_state, land_mask, layer_count)


def spread(value, work_ref, out_ref, group, zero):
    span, width = value.shape
    out_ref[group, :, 0:width] = value.astype(BF16)
    for tile in range(width // 128):
        work_ref[tile, 0:span, :] = value[:, 128 * tile : 128 * tile + 128]
    for shift in range(1, 5):
        for tile in range(width // 128):
            base = shift * width + 128 * tile
            out_ref[group, :, base : base + 128] = work_ref[
                tile, pl.ds(zero + shift, span), :
            ].astype(BF16)


def conv_layer(refs, raw_ref, sea_ref, work_ref, zero, layer, groups):
    in_ref, weight_ref, bias_ref, out_ref = refs
    width = weight_ref.shape[1]

    def activate(group):
        half = 0.5 * (raw_ref[:, 0:width] + bias_ref[...])
        value = half + half * jnp.tanh(half)
        if layer:
            row_of = lax.broadcasted_iota(jnp.int32, (128, width), 0)
            lane_of = lax.broadcasted_iota(jnp.int32, (128, width), 1)
            wanted = 4 * group + 2 * (layer + 1) + lane_of // (width // 4)
            pick = jnp.where(row_of == wanted, 1.0, 0.0).astype(BF16)
            value = value * jnp.dot(sea_ref[layer - 1], pick, preferred_element_type=F32)
        spread(value, work_ref, out_ref, group, zero)

    def body(group, carry):
        activate(jnp.maximum(group - 1, 0))
        lhs = jnp.concatenate([in_ref[group], in_ref[group + 1]], axis=1)
        raw_ref[:, 0:width] = jnp.dot(lhs, weight_ref[...], preferred_element_type=F32)
        return carry

    lax.fori_loop(0, groups, body, 0)
    activate(groups - 1)


def device_means(received):
    total = jnp.sum(received, axis=0, keepdims=True)
    column = jnp.transpose(jnp.broadcast_to(total, (128, 128)))
    counts = jnp.maximum(column[16:24], 1.0)
    return column[0:8] / counts, column[8:16] / counts


def step_kernel(*refs, step):
    first, last = step == 0, step == STEPS - 1
    margin = MARGINS[step]
    span = COLS + 2 * margin
    refs = list(refs)
    start_ref = refs.pop(0)
    own_ref, top_ref, bottom_ref = refs[:3]
    refs = refs[3:]
    if first:
        left_ref, right_ref = refs[:2]
        refs = refs[2:]
    else:
        recv_ref, wet_ref, sea_turned_ref = refs[:3]
        refs = refs[3:]
    w1_ref, w2_ref, w3_ref, w4_ref, b1_ref, b2_ref, b3_ref, new_ref, pay_ref = refs[:9]
    refs = refs[9:]
    if first:
        wet_ref, sea_turned_ref = refs[:2]
        refs = refs[2:]
    if last:
        raw_out_ref = refs.pop(0)
    else:
        send_up_ref, send_down_ref = refs[:2]
        refs = refs[2:]
    state_ref, a0_ref, a1_ref, a2_ref, a3_ref, work_ref, raw_ref, sea_ref, sum_ref = refs
    zero = start_ref[1]

    if first:
        lane = lax.broadcasted_iota(jnp.int32, (ROWS * 32, 128), 1)
        sides = jnp.where(lane < SIDE, right_ref[...].astype(F32), left_ref[...].astype(F32))
        state_ref[HALO : HALO + ROWS, :, 0:COLS] = own_ref[...]
        state_ref[HALO : HALO + ROWS, :, COLS:WIDE] = sides.reshape(ROWS, 32, 128)
        state_ref[0:HALO] = top_ref[...].astype(F32).reshape(HALO, 32, WIDE)
        state_ref[HALO + ROWS :] = bottom_ref[...].astype(F32).reshape(HALO, 32, WIDE)
        levels = jnp.broadcast_to(state_ref[:, 24:25, :], (EXT_ROWS, 8, WIDE))
        level_of = lax.broadcasted_iota(jnp.int32, levels.shape, 1).astype(F32)
        wet_ref[...] = jnp.where(level_of < levels, 1.0, 0.0)
        by_row = jnp.where(state_ref[:, 24, :] > 0.0, 1.0, 0.0)
        turned = jnp.transpose(
            jnp.concatenate([by_row, jnp.zeros((128 - EXT_ROWS, WIDE), F32)], axis=0)
        )
        sea_turned_ref[0:SIDE, :] = turned[WIDE - SIDE :]
        sea_turned_ref[SIDE:WIDE, :] = turned[0 : WIDE - SIDE]
        sea_turned_ref[WIDE:, :] = jnp.zeros((8, 128), F32)
    else:
        state_ref[HALO : HALO + ROWS, 0:24, :] = own_ref[...]
        state_ref[0:HALO, 0:24, :] = top_ref[...].astype(F32).reshape(HALO, 24, WIDE)
        state_ref[HALO + ROWS :, 0:24, :] = bottom_ref[...].astype(F32).reshape(HALO, 24, WIDE)
        zonal_mean, merid_mean = device_means(recv_ref[...])
        for base, mean in ((0, zonal_mean), (8, merid_mean)):
            scaled = jnp.concatenate([TIME_STEP * mean] * 3, axis=1)
            state_ref[:, base : base + 8, :] = (
                state_ref[:, base : base + 8, :] - scaled[None] * wet_ref[...]
            )
    first_channel = lax.broadcasted_iota(jnp.int32, (EXT_ROWS, 8, WIDE), 1) == 0
    state_ref[:, 24:32, :] = jnp.where(first_channel, 1.0 - wet_ref[...], 0.0)
    for layer in (1, 2):
        begin = SIDE - margin + 2 * (layer + 1)
        sea_ref[layer - 1] = sea_turned_ref[begin : begin + span, :].astype(BF16)

    work_ref[:, span:, :] = jnp.zeros((4, 8, 128), F32)
    for group in range(8):
        flat = state_ref[4 * group : 4 * group + 4].reshape(128, WIDE)
        turned = jnp.transpose(flat)
        around = jnp.concatenate([turned[WIDE - margin :], turned[0 : COLS + margin]], axis=0)
        spread(around, work_ref, a0_ref, group, zero)
    for layer, refs in enumerate(
        (
            (a0_ref, w1_ref, b1_ref, a1_ref),
            (a1_ref, w2_ref, b2_ref, a2_ref),
            (a2_ref, w3_ref, b3_ref, a3_ref),
        )
    ):
        conv_layer(refs, sum_ref, sea_ref, work_ref, zero, layer, 7 - layer)
    left = margin - HALO
    count = COLS + 2 * left
    lhs = jnp.concatenate([a3_ref[group, 0:count, :] for group in range(5)], axis=1)
    found = jnp.dot(lhs, w4_ref[...], preferred_element_type=F32)
    around = [found[left:], jnp.zeros((WIDE - count, 256), F32)]
    if left:
        around.append(found[:left])
    raw_ref[...] = jnp.transpose(jnp.concatenate(around, axis=0)).reshape(ROWS, 16, WIDE)

    def shifted_difference(field):
        return (pltpu.roll(field, WIDE - 1, 2) - pltpu.roll(field, 1, 2)) * 0.5

    rows = ROWS + 2
    low = HALO - 1
    zonal = state_ref[low : low + rows, 0:8, :]
    merid_above = state_ref[low + 1 : low + 1 + rows, 8:16, :]
    merid_below = state_ref[low - 1 : low - 1 + rows, 8:16, :]
    divergence = shifted_difference(zonal) + (merid_above - merid_below) * 0.5
    thickness = state_ref[low : low + rows, 16:24, :]
    h_new = (thickness - TIME_STEP * divergence) * wet_ref[low : low + rows]
    level = lax.broadcasted_iota(jnp.int32, (1, 8, 1), 1)
    pressure = None
    for other in range(LEVELS):
        weight = 0.5 + 0.1 * jnp.minimum(level, other).astype(F32)
        term = weight * h_new[:, other : other + 1, :]
        pressure = term if pressure is None else pressure + term
    grad_x = shifted_difference(pressure[1:-1])
    grad_y = (pressure[2:] - pressure[:-2]) * 0.5
    wet = wet_ref[HALO : HALO + ROWS]
    zonal_mid = state_ref[HALO : HALO + ROWS, 0:8, :]
    merid_mid = state_ref[HALO : HALO + ROWS, 8:16, :]
    global_row = start_ref[0] + lax.broadcasted_iota(jnp.int32, (ROWS, 8, WIDE), 0)
    coriolis = 0.3 + 0.5 * global_row.astype(F32) / 512.0
    raw_zonal = raw_ref[:, 0:8, :]
    raw_merid = raw_ref[:, 8:16, :]
    zonal_new = (
        zonal_mid + TIME_STEP * (-grad_x + coriolis * merid_mid - DRAG * zonal_mid + raw_zonal)
    ) * wet
    merid_new = (
        merid_mid + TIME_STEP * (-grad_y - coriolis * zonal_mid - DRAG * merid_mid + raw_merid)
    ) * wet
    new_ref[:, 0:8, :] = zonal_new
    new_ref[:, 8:16, :] = merid_new
    new_ref[:, 16:24, :] = h_new[1:-1]
    if last:
        raw_out_ref[...] = raw_ref[...]
    else:
        flat = new_ref[...].reshape(ROWS * 24, WIDE).astype(BF16)
        send_down_ref[...] = flat[0 : HALO * 24]
        send_up_ref[...] = flat[(ROWS - HALO) * 24 :]

    def lanes_of(field):
        by_column = jnp.sum(field, axis=0)
        return by_column[:, 0:128] + by_column[:, 128:256]

    columns = jnp.concatenate(
        [
            lanes_of(raw_zonal * wet),
            lanes_of(raw_merid * wet),
            lanes_of(wet),
            jnp.zeros((104, 128), F32),
        ],
        axis=0,
    )
    row = jnp.sum(jnp.transpose(columns), axis=0, keepdims=True)
    pay_ref[...] = jnp.broadcast_to(row, (128, 128))


def ocean_network_step(step, args):
    first, last = step == 0, step == STEPS - 1
    span = COLS + 2 * MARGINS[step]
    outs = [
        jax.ShapeDtypeStruct((ROWS, 24, WIDE), F32),
        jax.ShapeDtypeStruct((128, 128), F32),
    ]
    if first:
        outs.append(jax.ShapeDtypeStruct((EXT_ROWS, LEVELS, WIDE), F32))
        outs.append(jax.ShapeDtypeStruct((WIDE + 8, 128), F32))
    if last:
        outs.append(jax.ShapeDtypeStruct((ROWS, 16, WIDE), F32))
    else:
        outs += [jax.ShapeDtypeStruct((HALO * 24, WIDE), BF16)] * 2
    vmem = pl.BlockSpec(memory_space=pltpu.VMEM)
    return pl.pallas_call(
        functools.partial(step_kernel, step=step),
        out_shape=outs,
        in_specs=[pl.BlockSpec(memory_space=pltpu.SMEM)] + [vmem] * (len(args) - 1),
        out_specs=[vmem] * len(outs),
        scratch_shapes=[
            pltpu.VMEM((EXT_ROWS, 32, WIDE), F32),
            pltpu.VMEM((8, span, 5 * 128), BF16),
            pltpu.VMEM((7, span, 5 * 512), BF16),
            pltpu.VMEM((6, span, 5 * 256), BF16),
            pltpu.VMEM((5, span, 5 * 128), BF16),
            pltpu.VMEM((4, span + 8, 128), F32),
            pltpu.VMEM((ROWS, 16, WIDE), F32),
            pltpu.VMEM((2, span, 128), BF16),
            pltpu.VMEM((span, 512), F32),
        ],
        compiler_params=pltpu.CompilerParams(vmem_limit_bytes=40 * 2**20),
        name=f"step_{step}",
    )(*args)


def finish_kernel(recv_ref, state_ref, raw_ref, wet_ref, final_ref, forcing_ref, work_ref):
    zonal_mean, merid_mean = device_means(recv_ref[...])
    wet = wet_ref[HALO : HALO + ROWS, :, 0:COLS]
    zonal_mean = jnp.concatenate([zonal_mean] * 2, axis=1)[None]
    merid_mean = jnp.concatenate([merid_mean] * 2, axis=1)[None]
    work_ref[:, 0:8, :] = (raw_ref[:, 0:8, 0:COLS] - zonal_mean) * wet
    work_ref[:, 8:16, :] = (raw_ref[:, 8:16, 0:COLS] - merid_mean) * wet
    for channel in range(16):
        forcing_ref[channel] = work_ref[:, channel, :]
    work_ref[:, 0:8, :] = state_ref[:, 0:8, 0:COLS] - TIME_STEP * zonal_mean * wet
    work_ref[:, 8:16, :] = state_ref[:, 8:16, 0:COLS] - TIME_STEP * merid_mean * wet
    for channel in range(16):
        final_ref[channel] = work_ref[:, channel, :]
    for channel in range(16, 24):
        final_ref[channel] = state_ref[:, channel, 0:COLS]


def finish(received, state, raw, wet):
    return pl.pallas_call(
        finish_kernel,
        out_shape=[
            jax.ShapeDtypeStruct((24, ROWS, COLS), F32),
            jax.ShapeDtypeStruct((16, ROWS, COLS), F32),
        ],
        scratch_shapes=[pltpu.VMEM((ROWS, 16, COLS), F32)],
        compiler_params=pltpu.CompilerParams(vmem_limit_bytes=24 * 2**20),
        name="finish",
    )(received, state, raw, wet)


def both_ways(axis, up, down):
    count = lax.axis_size(axis)
    forward = [(i, i + 1) for i in range(count - 1)]
    backward = [(target, source) for source, target in forward]
    return lax.ppermute(up, axis, forward), lax.ppermute(down, axis, backward)


def local(
    ocean_state,
    land_mask,
    layer_count,
    conv1_weight,
    conv1_bias,
    conv2_weight,
    conv2_bias,
    conv3_weight,
    conv3_bias,
    conv4_weight,
):
    state, send_left, send_right = prepare(ocean_state, land_mask, layer_count)
    left, right = both_ways("sec", send_right, send_left)
    weights = banded(
        [conv1_weight, conv2_weight, conv3_weight, conv4_weight],
        [conv1_bias, conv2_bias, conv3_bias],
    )
    lane = lax.broadcasted_iota(jnp.int32, left.shape, 1)
    sides = jnp.where(lane < SIDE, right, left)
    whole = jnp.concatenate([send_left, send_right, sides], axis=1)
    halos = both_ways("lat", whole[HALO * 32 :], whole[: HALO * 32])

    start = (lax.axis_index("lat") * ROWS).astype(jnp.int32)
    start = jnp.stack([start, jnp.zeros((), jnp.int32)])
    extras = [left, right]
    for step in range(STEPS):
        results = ocean_network_step(step, [start, state, *halos, *extras, *weights])
        state = results[0]
        if step == 0:
            wet, sea = results[2:4]
        if step < STEPS - 1:
            halos = both_ways("lat", results[-2], results[-1])
        received = lax.all_to_all(results[1], ("sec", "lat"), 0, 0)
        extras = [received, wet, sea]
    return finish(received, state, results[2], wet)


def solution(mesh):
    return jax.shard_map(
        local,
        mesh=mesh,
        in_specs=(
            P(None, "lat", "sec"),
            P("lat", "sec"),
            P("lat", "sec"),
            P(),
            P(),
            P(),
            P(),
            P(),
            P(),
            P(),
        ),
        out_specs=(P(None, "lat", "sec"), P(None, "lat", "sec")),
        check_vma=False,
    )
```

```python
import functools

import jax
import jax.numpy as jnp
from jax import lax
from jax.experimental import pallas as pl
from jax.experimental.pallas import tpu as pltpu
from jax.sharding import PartitionSpec as P

LEVELS = 8
STEPS = 4
HALO = 8
TIME_STEP = 0.3
DRAG = 0.05
ROWS = 16
COLS = 256
EXT_ROWS = ROWS + 2 * HALO
WIDE = COLS + 128
SIDE = 64
MARGINS = tuple(HALO * (STEPS - step) for step in range(STEPS))
LAND_OFFSET = -(2.0**24)
PADDED = (32, 128, 64, 32)
F32 = jnp.float32
BF16 = jnp.bfloat16


def banded_kernel(*refs):
    weight_refs, bias_refs, band_refs, row_refs = refs[:4], refs[4:7], refs[7:11], refs[11:14]
    flat_ref, turned_ref = refs[14:]
    for layer in range(4):
        weight_ref, band_ref = weight_refs[layer], band_refs[layer]
        out_width = weight_ref.shape[1]
        in_width = weight_ref.shape[2] // 5
        in_pad = PADDED[layer]
        groups = band_ref.shape[0] // (20 * in_pad)
        out_rows = band_ref.shape[1] // out_width
        wide = -(-5 * in_width // 128) * 128
        flat_ref[...] = jnp.zeros(flat_ref.shape, F32)
        for offset in range(5):
            flat_ref[0:out_width, 0 : 5 * in_width] = weight_ref[offset].astype(F32)
            turned_ref[offset, 0:wide, :] = jnp.transpose(flat_ref[:, 0:wide])
        extra = in_pad - in_width
        for group in range(groups):
            for shift in range(5):
                for row in range(4):
                    parts = []
                    for out_row in range(out_rows):
                        offset = 4 * group + row - out_row
                        if not 0 <= offset < 5:
                            parts.append(jnp.zeros((in_pad, out_width), F32))
                            continue
                        part = turned_ref[
                            offset, shift * in_width : (shift + 1) * in_width, 0:out_width
                        ]
                        if extra:
                            pad = jnp.zeros((extra, out_width), F32)
                            if layer == 0 and offset == 2 and shift == 2:
                                first = lax.broadcasted_iota(jnp.int32, pad.shape, 0) == 0
                                pad = jnp.where(first, LAND_OFFSET, 0.0)
                            part = jnp.concatenate([part, pad], axis=0)
                        parts.append(part)
                    base = ((group * 5 + shift) * 4 + row) * in_pad
                    band_ref[base : base + in_pad, :] = jnp.concatenate(parts, axis=1).astype(BF16)
    for bias_ref, row_ref in zip(bias_refs, row_refs):
        row_ref[...] = jnp.concatenate([bias_ref[...]] * 4, axis=1)


def banded(weights, biases):
    shapes = [(1280, 512), (5120, 256), (2560, 128), (3200, 256)]
    outs = [jax.ShapeDtypeStruct(shape, BF16) for shape in shapes]
    outs += [jax.ShapeDtypeStruct((1, width), F32) for width in (512, 256, 128)]
    return pl.pallas_call(
        banded_kernel,
        out_shape=outs,
        scratch_shapes=[pltpu.VMEM((128, 640), F32), pltpu.VMEM((5, 640, 128), F32)],
        compiler_params=pltpu.CompilerParams(vmem_limit_bytes=24 * 2**20),
        name="banded",
    )(*weights, *[bias[None] for bias in biases])


def lanes_between(shape, low, high):
    lane = lax.broadcasted_iota(jnp.int32, shape, 1)
    return (lane >= low) & (lane < high)


def fold_edge(tile, low):
    height = tile.shape[0] // 4
    folded = tile[0:height]
    for part in range(1, 4):
        moved = pltpu.roll(tile[part * height : (part + 1) * height], 32 * part, 1)
        begin = (low + 32 * part) % 128
        folded = jnp.where(lanes_between(moved.shape, begin, begin + 32), moved, folded)
    return folded


def unfold_edge(folded):
    parts = [folded] + [pltpu.roll(folded, 128 - 32 * part, 1) for part in range(1, 4)]
    return jnp.concatenate(parts, axis=0)


def fold_sides(sides):
    height = sides.shape[0] // 2
    moved = pltpu.roll(sides[height:], 64, 1)
    both = jnp.where(lanes_between(moved.shape, 32, 96), moved, sides[:height])
    return jnp.concatenate([both[: height // 2], both[height // 2 :]], axis=1)


def unfold_sides(folded):
    both = jnp.concatenate([folded[:, 0:128], folded[:, 128:256]], axis=0)
    return jnp.concatenate([both, pltpu.roll(both, 64, 1)], axis=0)


def pack_rows(flat):
    return jnp.concatenate([flat[:, 0:COLS], fold_sides(flat[:, COLS:])], axis=0)


def unpack_rows(packed, state_ref, low):
    height = HALO * 24
    fields = packed[0 : height + height // 4].astype(F32)
    state_ref[low : low + HALO, 0:24, 0:COLS] = fields[0:height].reshape(HALO, 24, COLS)
    state_ref[low : low + HALO, 0:24, COLS:WIDE] = unfold_sides(fields[height:]).reshape(
        HALO, 24, 128
    )


def prepare_kernel(state_ref, land_ref, count_ref, own_ref, left_ref, right_ref):
    levels = land_ref[...] * count_ref[...]
    own_ref[:, 24:32, :] = jnp.zeros((ROWS, 8, COLS), F32)
    own_ref[:, 24, :] = levels.astype(F32)
    for channel in range(24):
        wet = jnp.where(levels > channel % LEVELS, 1.0, 0.0)
        own_ref[:, channel, :] = state_ref[channel] * wet
    flat = own_ref[...].reshape(ROWS * 32, COLS)
    left_ref[...] = fold_edge(flat[:, 0:128], 0).astype(BF16)
    right_ref[...] = fold_edge(flat[:, COLS - 128 :], 96).astype(BF16)


def small_params():
    return pltpu.CompilerParams(vmem_limit_bytes=24 * 2**20)


def prepare(ocean_state, land_mask, layer_count):
    return pl.pallas_call(
        prepare_kernel,
        out_shape=[jax.ShapeDtypeStruct((ROWS, 32, COLS), F32)]
        + [jax.ShapeDtypeStruct((ROWS * 8, 128), BF16)] * 2,
        compiler_params=small_params(),
        name="prepare",
    )(ocean_state, land_mask, layer_count)


def pack_kernel(own_ref, left_ref, right_ref, wide_ref, up_ref, down_ref):
    right = unfold_edge(right_ref[...].astype(F32))
    left = unfold_edge(left_ref[...].astype(F32))
    sides = jnp.where(lanes_between(left.shape, 0, SIDE), right, left)
    wide_ref[:, :, 0:COLS] = own_ref[...]
    wide_ref[:, :, COLS:WIDE] = sides.reshape(ROWS, 32, 128)
    for low, out_ref in ((0, down_ref), (ROWS - HALO, up_ref)):
        fields = wide_ref[low : low + HALO, 0:24, :].reshape(HALO * 24, WIDE)
        levels = wide_ref[low : low + HALO, 24, :]
        rest = jnp.concatenate([levels[:, COLS:], jnp.zeros((HALO, 128), F32)], axis=1)
        out_ref[...] = jnp.concatenate(
            [pack_rows(fields), levels[:, 0:COLS], rest], axis=0
        ).astype(BF16)


def pack(own, left, right):
    return pl.pallas_call(
        pack_kernel,
        out_shape=[jax.ShapeDtypeStruct((ROWS, 32, WIDE), F32)]
        + [jax.ShapeDtypeStruct((HALO * 32, COLS), BF16)] * 2,
        compiler_params=small_params(),
        name="pack",
    )(own, left, right)


def spread(value, work_ref, out_ref, group, zero):
    span, width = value.shape
    out_ref[group, :, 0:width] = value.astype(BF16)
    for tile in range(width // 128):
        work_ref[tile, 0:span, :] = value[:, 128 * tile : 128 * tile + 128]
    for shift in range(1, 5):
        for tile in range(width // 128):
            base = shift * width + 128 * tile
            out_ref[group, :, base : base + 128] = work_ref[
                tile, pl.ds(zero + shift, span), :
            ].astype(BF16)


def conv_layer(refs, raw_ref, sea_ref, work_ref, zero, layer, groups):
    in_ref, weight_ref, bias_ref, out_ref = refs
    width = weight_ref.shape[1]

    def activate(group):
        half = 0.5 * (raw_ref[:, 0:width] + bias_ref[...])
        value = half + half * jnp.tanh(half)
        if layer:
            row_of = lax.broadcasted_iota(jnp.int32, (128, width), 0)
            lane_of = lax.broadcasted_iota(jnp.int32, (128, width), 1)
            wanted = 4 * group + 2 * (layer + 1) + lane_of // (width // 4)
            pick = jnp.where(row_of == wanted, 1.0, 0.0).astype(BF16)
            value = value * jnp.dot(sea_ref[layer - 1], pick, preferred_element_type=F32)
        spread(value, work_ref, out_ref, group, zero)

    def body(group, carry):
        activate(jnp.maximum(group - 1, 0))
        lhs = jnp.concatenate([in_ref[group], in_ref[group + 1]], axis=1)
        raw_ref[:, 0:width] = jnp.dot(lhs, weight_ref[...], preferred_element_type=F32)
        return carry

    lax.fori_loop(0, groups, body, 0)
    activate(groups - 1)


def device_means(received):
    total = jnp.sum(received, axis=0, keepdims=True)
    column = jnp.transpose(jnp.broadcast_to(total, (128, 128)))
    counts = jnp.maximum(column[16:24], 1.0)
    return column[0:8] / counts, column[8:16] / counts


def step_kernel(*refs, step):
    first, last = step == 0, step == STEPS - 1
    margin = MARGINS[step]
    span = COLS + 2 * margin
    refs = list(refs)
    start_ref = refs.pop(0)
    own_ref, top_ref, bottom_ref = refs[:3]
    refs = refs[3:]
    if not first:
        recv_ref, wet_ref, sea_turned_ref = refs[:3]
        refs = refs[3:]
    w1_ref, w2_ref, w3_ref, w4_ref, b1_ref, b2_ref, b3_ref, new_ref, pay_ref = refs[:9]
    refs = refs[9:]
    if first:
        wet_ref, sea_turned_ref = refs[:2]
        refs = refs[2:]
    if last:
        raw_out_ref = refs.pop(0)
    else:
        send_up_ref, send_down_ref = refs[:2]
        refs = refs[2:]
    state_ref, a0_ref, a1_ref, a2_ref, a3_ref, work_ref, raw_ref, sea_ref, sum_ref = refs[:9]
    turn_ref = refs[9]
    zero = start_ref[1]

    halves = ((top_ref, 0), (bottom_ref, HALO + ROWS))
    for packed_ref, low in halves:
        unpack_rows(packed_ref[...], state_ref, low)
    if first:
        state_ref[HALO : HALO + ROWS] = own_ref[...]
        for packed_ref, low in halves:
            levels = packed_ref[HALO * 30 :, :].astype(F32)
            state_ref[low : low + HALO, 24, 0:COLS] = levels[0:HALO]
            state_ref[low : low + HALO, 24, COLS:WIDE] = levels[HALO:, 0:128]
        levels = jnp.broadcast_to(state_ref[:, 24:25, :], (EXT_ROWS, 8, WIDE))
        level_of = lax.broadcasted_iota(jnp.int32, levels.shape, 1).astype(F32)
        wet_ref[...] = jnp.where(level_of < levels, 1.0, 0.0)
        by_row = jnp.where(state_ref[:, 24, :] > 0.0, 1.0, 0.0)
        turned = jnp.transpose(
            jnp.concatenate([by_row, jnp.zeros((128 - EXT_ROWS, WIDE), F32)], axis=0)
        )
        sea_turned_ref[0:SIDE, :] = turned[WIDE - SIDE :]
        sea_turned_ref[SIDE:WIDE, :] = turned[0 : WIDE - SIDE]
        sea_turned_ref[WIDE:, :] = jnp.zeros((8, 128), F32)
    else:
        state_ref[HALO : HALO + ROWS, 0:24, :] = own_ref[...]
        zonal_mean, merid_mean = device_means(recv_ref[...])
        for base, mean in ((0, zonal_mean), (8, merid_mean)):
            scaled = jnp.concatenate([TIME_STEP * mean] * 3, axis=1)
            state_ref[:, base : base + 8, :] = (
                state_ref[:, base : base + 8, :] - scaled[None] * wet_ref[...]
            )
    first_channel = lax.broadcasted_iota(jnp.int32, (EXT_ROWS, 8, WIDE), 1) == 0
    state_ref[:, 24:32, :] = jnp.where(first_channel, 1.0 - wet_ref[...], 0.0)
    for layer in (1, 2):
        begin = SIDE - margin + 2 * (layer + 1)
        sea_ref[layer - 1] = sea_turned_ref[begin : begin + span, :].astype(BF16)

    work_ref[:, span:, :] = jnp.zeros((4, 8, 128), F32)
    turn_ref[:, span:, :] = jnp.zeros((1, 8, 128), F32)

    def turn(group):
        flat = state_ref[4 * group : 4 * group + 4].reshape(128, WIDE)
        turned = jnp.transpose(flat)
        around = jnp.concatenate([turned[WIDE - margin :], turned[0 : COLS + margin]], axis=0)
        spread(around, turn_ref, a0_ref, group, zero)

    for group in range(8):
        turn(group)
    for layer, refs in enumerate(
        (
            (a0_ref, w1_ref, b1_ref, a1_ref),
            (a1_ref, w2_ref, b2_ref, a2_ref),
            (a2_ref, w3_ref, b3_ref, a3_ref),
        )
    ):
        conv_layer(refs, sum_ref, sea_ref, work_ref, zero, layer, 7 - layer)
    left = margin - HALO
    count = COLS + 2 * left
    lhs = jnp.concatenate([a3_ref[group, 0:count, :] for group in range(5)], axis=1)
    found = jnp.dot(lhs, w4_ref[...], preferred_element_type=F32)
    around = [found[left:], jnp.zeros((WIDE - count, 256), F32)]
    if left:
        around.append(found[:left])
    raw_ref[...] = jnp.transpose(jnp.concatenate(around, axis=0)).reshape(ROWS, 16, WIDE)

    def shifted_difference(field):
        return (pltpu.roll(field, WIDE - 1, 2) - pltpu.roll(field, 1, 2)) * 0.5

    rows = ROWS + 2
    low = HALO - 1
    zonal = state_ref[low : low + rows, 0:8, :]
    merid_above = state_ref[low + 1 : low + 1 + rows, 8:16, :]
    merid_below = state_ref[low - 1 : low - 1 + rows, 8:16, :]
    divergence = shifted_difference(zonal) + (merid_above - merid_below) * 0.5
    thickness = state_ref[low : low + rows, 16:24, :]
    h_new = (thickness - TIME_STEP * divergence) * wet_ref[low : low + rows]
    level = lax.broadcasted_iota(jnp.int32, (1, 8, 1), 1)
    pressure = None
    for other in range(LEVELS):
        weight = 0.5 + 0.1 * jnp.minimum(level, other).astype(F32)
        term = weight * h_new[:, other : other + 1, :]
        pressure = term if pressure is None else pressure + term
    grad_x = shifted_difference(pressure[1:-1])
    grad_y = (pressure[2:] - pressure[:-2]) * 0.5
    wet = wet_ref[HALO : HALO + ROWS]
    zonal_mid = state_ref[HALO : HALO + ROWS, 0:8, :]
    merid_mid = state_ref[HALO : HALO + ROWS, 8:16, :]
    global_row = start_ref[0] + lax.broadcasted_iota(jnp.int32, (ROWS, 8, WIDE), 0)
    coriolis = 0.3 + 0.5 * global_row.astype(F32) / 512.0
    raw_zonal = raw_ref[:, 0:8, :]
    raw_merid = raw_ref[:, 8:16, :]
    zonal_new = (
        zonal_mid + TIME_STEP * (-grad_x + coriolis * merid_mid - DRAG * zonal_mid + raw_zonal)
    ) * wet
    merid_new = (
        merid_mid + TIME_STEP * (-grad_y - coriolis * zonal_mid - DRAG * merid_mid + raw_merid)
    ) * wet
    new_ref[:, 0:8, :] = zonal_new
    new_ref[:, 8:16, :] = merid_new
    new_ref[:, 16:24, :] = h_new[1:-1]
    if last:
        raw_out_ref[...] = raw_ref[...]
    else:
        flat = new_ref[...].reshape(ROWS * 24, WIDE)
        send_down_ref[...] = pack_rows(flat[0 : HALO * 24]).astype(BF16)
        send_up_ref[...] = pack_rows(flat[(ROWS - HALO) * 24 :]).astype(BF16)

    def lanes_of(field):
        by_column = jnp.sum(field, axis=0)
        return by_column[:, 0:128] + by_column[:, 128:256]

    columns = jnp.concatenate(
        [
            lanes_of(raw_zonal * wet),
            lanes_of(raw_merid * wet),
            lanes_of(wet),
            jnp.zeros((104, 128), F32),
        ],
        axis=0,
    )
    row = jnp.sum(jnp.transpose(columns), axis=0, keepdims=True)
    pay_ref[...] = jnp.broadcast_to(row, (128, 128))


def ocean_network_step(step, args):
    first, last = step == 0, step == STEPS - 1
    span = COLS + 2 * MARGINS[step]
    outs = [
        jax.ShapeDtypeStruct((ROWS, 24, WIDE), F32),
        jax.ShapeDtypeStruct((128, 128), F32),
    ]
    if first:
        outs.append(jax.ShapeDtypeStruct((EXT_ROWS, LEVELS, WIDE), F32))
        outs.append(jax.ShapeDtypeStruct((WIDE + 8, 128), F32))
    if last:
        outs.append(jax.ShapeDtypeStruct((ROWS, 16, WIDE), F32))
    else:
        outs += [jax.ShapeDtypeStruct((HALO * 30, COLS), BF16)] * 2
    vmem = pl.BlockSpec(memory_space=pltpu.VMEM)
    return pl.pallas_call(
        functools.partial(step_kernel, step=step),
        out_shape=outs,
        in_specs=[pl.BlockSpec(memory_space=pltpu.SMEM)] + [vmem] * (len(args) - 1),
        out_specs=[vmem] * len(outs),
        scratch_shapes=[
            pltpu.VMEM((EXT_ROWS, 32, WIDE), F32),
            pltpu.VMEM((8, span, 5 * 128), BF16),
            pltpu.VMEM((7, span, 5 * 512), BF16),
            pltpu.VMEM((6, span, 5 * 256), BF16),
            pltpu.VMEM((5, span, 5 * 128), BF16),
            pltpu.VMEM((4, span + 8, 128), F32),
            pltpu.VMEM((ROWS, 16, WIDE), F32),
            pltpu.VMEM((2, span, 128), BF16),
            pltpu.VMEM((span, 512), F32),
            pltpu.VMEM((1, span + 8, 128), F32),
        ],
        compiler_params=pltpu.CompilerParams(vmem_limit_bytes=40 * 2**20),
        name=f"step_{step}",
    )(*args)


def finish_kernel(recv_ref, state_ref, raw_ref, wet_ref, final_ref, forcing_ref, work_ref):
    zonal_mean, merid_mean = device_means(recv_ref[...])
    wet = wet_ref[HALO : HALO + ROWS, :, 0:COLS]
    zonal_mean = jnp.concatenate([zonal_mean] * 2, axis=1)[None]
    merid_mean = jnp.concatenate([merid_mean] * 2, axis=1)[None]
    work_ref[:, 0:8, :] = (raw_ref[:, 0:8, 0:COLS] - zonal_mean) * wet
    work_ref[:, 8:16, :] = (raw_ref[:, 8:16, 0:COLS] - merid_mean) * wet
    for channel in range(16):
        forcing_ref[channel] = work_ref[:, channel, :]
    work_ref[:, 0:8, :] = state_ref[:, 0:8, 0:COLS] - TIME_STEP * zonal_mean * wet
    work_ref[:, 8:16, :] = state_ref[:, 8:16, 0:COLS] - TIME_STEP * merid_mean * wet
    for channel in range(16):
        final_ref[channel] = work_ref[:, channel, :]
    for channel in range(16, 24):
        final_ref[channel] = state_ref[:, channel, 0:COLS]


def finish(received, state, raw, wet):
    return pl.pallas_call(
        finish_kernel,
        out_shape=[
            jax.ShapeDtypeStruct((24, ROWS, COLS), F32),
            jax.ShapeDtypeStruct((16, ROWS, COLS), F32),
        ],
        scratch_shapes=[pltpu.VMEM((ROWS, 16, COLS), F32)],
        compiler_params=pltpu.CompilerParams(vmem_limit_bytes=24 * 2**20),
        name="finish",
    )(received, state, raw, wet)


def both_ways(axis, up, down):
    count = lax.axis_size(axis)
    forward = [(i, i + 1) for i in range(count - 1)]
    backward = [(target, source) for source, target in forward]
    return lax.ppermute(up, axis, forward), lax.ppermute(down, axis, backward)


def local(
    ocean_state,
    land_mask,
    layer_count,
    conv1_weight,
    conv1_bias,
    conv2_weight,
    conv2_bias,
    conv3_weight,
    conv3_bias,
    conv4_weight,
):
    state, send_left, send_right = prepare(ocean_state, land_mask, layer_count)
    left, right = both_ways("sec", send_right, send_left)
    weights = banded(
        [conv1_weight, conv2_weight, conv3_weight, conv4_weight],
        [conv1_bias, conv2_bias, conv3_bias],
    )
    state, send_up, send_down = pack(state, left, right)
    halos = both_ways("lat", send_up, send_down)

    start = (lax.axis_index("lat") * ROWS).astype(jnp.int32)
    start = jnp.stack([start, jnp.zeros((), jnp.int32)])
    extras = []
    for step in range(STEPS):
        results = ocean_network_step(step, [start, state, *halos, *extras, *weights])
        state = results[0]
        if step == 0:
            wet, sea = results[2:4]
        if step < STEPS - 1:
            halos = both_ways("lat", results[-2], results[-1])
        received = lax.all_to_all(results[1], ("sec", "lat"), 0, 0)
        extras = [received, wet, sea]
    return finish(received, state, results[2], wet)


def solution(mesh):
    return jax.shard_map(
        local,
        mesh=mesh,
        in_specs=(
            P(None, "lat", "sec"),
            P("lat", "sec"),
            P("lat", "sec"),
            P(),
            P(),
            P(),
            P(),
            P(),
            P(),
            P(),
        ),
        out_specs=(P(None, "lat", "sec"), P(None, "lat", "sec")),
        check_vma=False,
    )
```

```python
import functools

import jax
import jax.numpy as jnp
from jax import lax
from jax.experimental import pallas as pl
from jax.experimental.pallas import tpu as pltpu
from jax.sharding import PartitionSpec as P

LEVELS = 8
STEPS = 4
HALO = 8
TIME_STEP = 0.3
DRAG = 0.05
ROWS = 16
COLS = 256
EXT_ROWS = ROWS + 2 * HALO
WIDE = COLS + 128
SIDE = 64
MARGINS = tuple(HALO * (STEPS - step) for step in range(STEPS))
LAND_OFFSET = -(2.0**24)
PADDED = (32, 128, 64, 32)
F32 = jnp.float32
BF16 = jnp.bfloat16


def banded_kernel(*refs):
    sources, band_refs, row_refs = refs[:7], refs[8:12], refs[12:15]
    copies, (flat_ref, turned_ref, sems) = refs[15:22], refs[22:]
    fetch = [
        pltpu.make_async_copy(source, copy, sems.at[index])
        for index, (source, copy) in enumerate(zip(sources, copies))
    ]
    for one in fetch:
        one.start()
    for one in fetch:
        one.wait()
    weight_refs, bias_refs = copies[:4], copies[4:]
    for layer in range(4):
        weight_ref, band_ref = weight_refs[layer], band_refs[layer]
        turned_already = layer == 0
        out_width = weight_ref.shape[2 if turned_already else 1]
        in_width = weight_ref.shape[1 if turned_already else 2] // 5
        in_pad = PADDED[layer]
        groups = band_ref.shape[0] // (20 * in_pad)
        out_rows = band_ref.shape[1] // out_width
        wide = -(-5 * in_width // 128) * 128
        flat_ref[...] = jnp.zeros(flat_ref.shape, F32)
        for offset in range(5):
            if turned_already:
                turned_ref[offset, 0 : 5 * in_width, 0:out_width] = weight_ref[offset].astype(F32)
                continue
            flat_ref[0:out_width, 0 : 5 * in_width] = weight_ref[offset].astype(F32)
            turned_ref[offset, 0:wide, :] = jnp.transpose(flat_ref[:, 0:wide])
        extra = in_pad - in_width
        for group in range(groups):
            for shift in range(5):
                for row in range(4):
                    parts = []
                    for out_row in range(out_rows):
                        offset = 4 * group + row - out_row
                        if not 0 <= offset < 5:
                            parts.append(jnp.zeros((in_pad, out_width), F32))
                            continue
                        part = turned_ref[
                            offset, shift * in_width : (shift + 1) * in_width, 0:out_width
                        ]
                        if extra:
                            pad = jnp.zeros((extra, out_width), F32)
                            if layer == 0 and offset == 2 and shift == 2:
                                first = lax.broadcasted_iota(jnp.int32, pad.shape, 0) == 0
                                pad = jnp.where(first, LAND_OFFSET, 0.0)
                            part = jnp.concatenate([part, pad], axis=0)
                        parts.append(part)
                    base = ((group * 5 + shift) * 4 + row) * in_pad
                    band_ref[base : base + in_pad, :] = jnp.concatenate(parts, axis=1).astype(BF16)
    for bias_ref, row_ref in zip(bias_refs, row_refs):
        row_ref[...] = jnp.concatenate([bias_ref[...]] * 4, axis=1)


def banded(weights, biases, after):
    shapes = [(1280, 512), (5120, 256), (2560, 128), (3200, 256)]
    outs = [jax.ShapeDtypeStruct(shape, BF16) for shape in shapes]
    outs += [jax.ShapeDtypeStruct((1, width), F32) for width in (512, 256, 128)]
    first, *others = weights
    args = [first.transpose(0, 2, 1), *others, *[bias[None] for bias in biases]]
    return pl.pallas_call(
        banded_kernel,
        out_shape=outs,
        in_specs=[pl.BlockSpec(memory_space=pltpu.HBM)] * 7 + [pl.BlockSpec(memory_space=pl.ANY)],
        scratch_shapes=[pltpu.VMEM(arg.shape, arg.dtype) for arg in args]
        + [
            pltpu.VMEM((128, 640), F32),
            pltpu.VMEM((5, 640, 128), F32),
            pltpu.SemaphoreType.DMA((7,)),
        ],
        compiler_params=small_params(),
        name="banded",
    )(*args, after)


def lanes_between(shape, low, high):
    lane = lax.broadcasted_iota(jnp.int32, shape, 1)
    return (lane >= low) & (lane < high)


def fold_edge(tile, low):
    height = tile.shape[0] // 4
    folded = tile[0:height]
    for part in range(1, 4):
        moved = pltpu.roll(tile[part * height : (part + 1) * height], 32 * part, 1)
        begin = (low + 32 * part) % 128
        folded = jnp.where(lanes_between(moved.shape, begin, begin + 32), moved, folded)
    return folded


def unfold_edge(folded):
    parts = [folded] + [pltpu.roll(folded, 128 - 32 * part, 1) for part in range(1, 4)]
    return jnp.concatenate(parts, axis=0)


def fold_sides(sides):
    height = sides.shape[0] // 2
    moved = pltpu.roll(sides[height:], 64, 1)
    both = jnp.where(lanes_between(moved.shape, 32, 96), moved, sides[:height])
    return jnp.concatenate([both[: height // 2], both[height // 2 :]], axis=1)


def unfold_sides(folded):
    both = jnp.concatenate([folded[:, 0:128], folded[:, 128:256]], axis=0)
    return jnp.concatenate([both, pltpu.roll(both, 64, 1)], axis=0)


def pack_rows(flat):
    return jnp.concatenate([flat[:, 0:COLS], fold_sides(flat[:, COLS:])], axis=0)


def unpack_rows(packed, state_ref, low):
    height = HALO * 24
    fields = packed[0 : height + height // 4].astype(F32)
    state_ref[low : low + HALO, 0:24, 0:COLS] = fields[0:height].reshape(HALO, 24, COLS)
    state_ref[low : low + HALO, 0:24, COLS:WIDE] = unfold_sides(fields[height:]).reshape(
        HALO, 24, 128
    )


def prepare_kernel(*refs):
    sources, (own_ref, left_ref, right_ref), copies, sems = refs[:3], refs[3:6], refs[6:9], refs[9]
    fetch = [
        pltpu.make_async_copy(source, copy, sems.at[index])
        for index, (source, copy) in enumerate(zip(sources, copies))
    ]
    for one in fetch:
        one.start()
    for one in fetch:
        one.wait()
    state_ref, land_ref, count_ref = copies
    levels = land_ref[...] * count_ref[...]
    own_ref[:, 24:32, :] = jnp.zeros((ROWS, 8, COLS), F32)
    own_ref[:, 24, :] = levels.astype(F32)
    for channel in range(24):
        wet = jnp.where(levels > channel % LEVELS, 1.0, 0.0)
        own_ref[:, channel, :] = state_ref[channel] * wet
    flat = own_ref[...].reshape(ROWS * 32, COLS)
    left_ref[...] = fold_edge(flat[:, 0:128], 0).astype(BF16)
    right_ref[...] = fold_edge(flat[:, COLS - 128 :], 96).astype(BF16)


def small_params():
    return pltpu.CompilerParams(vmem_limit_bytes=8 * 2**20)


def prepare(*args):
    return pl.pallas_call(
        prepare_kernel,
        out_shape=[jax.ShapeDtypeStruct((ROWS, 32, COLS), F32)]
        + [jax.ShapeDtypeStruct((ROWS * 8, 128), BF16)] * 2,
        in_specs=[pl.BlockSpec(memory_space=pltpu.HBM)] * 3,
        scratch_shapes=[pltpu.VMEM(arg.shape, arg.dtype) for arg in args]
        + [pltpu.SemaphoreType.DMA((3,))],
        compiler_params=small_params(),
        name="prepare",
    )(*args)


def pack_kernel(own_ref, left_ref, right_ref, wide_ref, up_ref, down_ref):
    right = unfold_edge(right_ref[...].astype(F32))
    left = unfold_edge(left_ref[...].astype(F32))
    sides = jnp.where(lanes_between(left.shape, 0, SIDE), right, left)
    wide_ref[:, :, 0:COLS] = own_ref[...]
    wide_ref[:, :, COLS:WIDE] = sides.reshape(ROWS, 32, 128)
    for low, out_ref in ((0, down_ref), (ROWS - HALO, up_ref)):
        fields = wide_ref[low : low + HALO, 0:24, :].reshape(HALO * 24, WIDE)
        levels = wide_ref[low : low + HALO, 24, :]
        rest = jnp.concatenate([levels[:, COLS:], jnp.zeros((HALO, 128), F32)], axis=1)
        out_ref[...] = jnp.concatenate(
            [pack_rows(fields), levels[:, 0:COLS], rest], axis=0
        ).astype(BF16)


def pack(own, left, right):
    return pl.pallas_call(
        pack_kernel,
        out_shape=[jax.ShapeDtypeStruct((ROWS, 32, WIDE), F32)]
        + [jax.ShapeDtypeStruct((HALO * 32, COLS), BF16)] * 2,
        compiler_params=small_params(),
        name="pack",
    )(own, left, right)


def spread(value, work_ref, out_ref, group, zero):
    span, width = value.shape
    out_ref[group, :, 0:width] = value.astype(BF16)
    for tile in range(width // 128):
        work_ref[tile, 0:span, :] = value[:, 128 * tile : 128 * tile + 128]
    for shift in range(1, 5):
        for tile in range(width // 128):
            base = shift * width + 128 * tile
            out_ref[group, :, base : base + 128] = work_ref[
                tile, pl.ds(zero + shift, span), :
            ].astype(BF16)


def conv_layer(refs, raw_ref, sea_ref, work_ref, zero, layer, groups, skip):
    in_ref, weight_ref, bias_ref, out_ref, mask_ref = refs
    span = in_ref.shape[1]
    width = weight_ref.shape[1]

    def activate(group):
        half = 0.5 * (raw_ref[:, 0:width] + bias_ref[...])
        value = half + half * jnp.tanh(half)
        if layer and sea_ref is not None:
            row_of = lax.broadcasted_iota(jnp.int32, (128, width), 0)
            lane_of = lax.broadcasted_iota(jnp.int32, (128, width), 1)
            wanted = 4 * group + 2 * (layer + 1) + lane_of // (width // 4)
            pick = jnp.where(row_of == wanted, 1.0, 0.0).astype(BF16)
            mask = jnp.dot(sea_ref[layer - 1], pick, preferred_element_type=F32)
            mask_ref[group] = mask
            value = value * mask
        elif layer:
            value = value * mask_ref[group, skip : skip + span, :]
        spread(value, work_ref, out_ref, group, zero)

    def body(group, carry):
        activate(jnp.maximum(group - 1, 0))
        lhs = jnp.concatenate([in_ref[group], in_ref[group + 1]], axis=1)
        raw_ref[:, 0:width] = jnp.dot(lhs, weight_ref[...], preferred_element_type=F32)
        return carry

    lax.fori_loop(0, groups, body, 0)
    activate(groups - 1)


def device_means(received):
    total = jnp.sum(received, axis=0, keepdims=True)
    column = jnp.transpose(jnp.broadcast_to(total, (128, 128)))
    counts = jnp.maximum(column[16:24], 1.0)
    return column[0:8] / counts, column[8:16] / counts


def step_kernel(*refs, step):
    first, last = step == 0, step == STEPS - 1
    margin = MARGINS[step]
    span = COLS + 2 * margin
    refs = list(refs)
    start_ref = refs.pop(0)
    own_ref, top_ref, bottom_ref = refs[:3]
    refs = refs[3:]
    if not first:
        recv_ref, wet_ref, mask2_ref, mask3_ref = refs[:4]
        refs = refs[4:]
    w1_ref, w2_ref, w3_ref, w4_ref, b1_ref, b2_ref, b3_ref, new_ref, pay_ref = refs[:9]
    refs = refs[9:]
    if first:
        wet_ref, mask2_ref, mask3_ref = refs[:3]
        refs = refs[3:]
    if last:
        raw_out_ref = refs.pop(0)
    else:
        send_up_ref, send_down_ref = refs[:2]
        refs = refs[2:]
    state_ref, a0_ref, a1_ref, a2_ref, a3_ref, work_ref, raw_ref, sea_ref, sum_ref = refs[:9]
    turn_ref = refs[9]
    sea_turned_ref = refs[10] if first else None
    zero = start_ref[1]

    halves = ((top_ref, 0), (bottom_ref, HALO + ROWS))
    for packed_ref, low in halves:
        unpack_rows(packed_ref[...], state_ref, low)
    if first:
        state_ref[HALO : HALO + ROWS] = own_ref[...]
        for packed_ref, low in halves:
            levels = packed_ref[HALO * 30 :, :].astype(F32)
            state_ref[low : low + HALO, 24, 0:COLS] = levels[0:HALO]
            state_ref[low : low + HALO, 24, COLS:WIDE] = levels[HALO:, 0:128]
        levels = jnp.broadcast_to(state_ref[:, 24:25, :], (EXT_ROWS, 8, WIDE))
        level_of = lax.broadcasted_iota(jnp.int32, levels.shape, 1).astype(F32)
        wet_ref[...] = jnp.where(level_of < levels, 1.0, 0.0)
        by_row = jnp.where(state_ref[:, 24, :] > 0.0, 1.0, 0.0)
        turned = jnp.transpose(
            jnp.concatenate([by_row, jnp.zeros((128 - EXT_ROWS, WIDE), F32)], axis=0)
        )
        sea_turned_ref[0:SIDE, :] = turned[WIDE - SIDE :]
        sea_turned_ref[SIDE:WIDE, :] = turned[0 : WIDE - SIDE]
        sea_turned_ref[WIDE:, :] = jnp.zeros((8, 128), F32)
    else:
        state_ref[HALO : HALO + ROWS, 0:24, :] = own_ref[...]
        zonal_mean, merid_mean = device_means(recv_ref[...])
        for base, mean in ((0, zonal_mean), (8, merid_mean)):
            scaled = jnp.concatenate([TIME_STEP * mean] * 3, axis=1)
            state_ref[:, base : base + 8, :] = (
                state_ref[:, base : base + 8, :] - scaled[None] * wet_ref[...]
            )
    first_channel = lax.broadcasted_iota(jnp.int32, (EXT_ROWS, 8, WIDE), 1) == 0
    state_ref[:, 24:32, :] = jnp.where(first_channel, 1.0 - wet_ref[...], 0.0)
    for layer in (1, 2) if first else ():
        begin = SIDE - margin + 2 * (layer + 1)
        sea_ref[layer - 1] = sea_turned_ref[begin : begin + span, :].astype(BF16)

    work_ref[:, span:, :] = jnp.zeros((4, 8, 128), F32)
    turn_ref[:, span:, :] = jnp.zeros((1, 8, 128), F32)

    def turn(group):
        flat = state_ref[4 * group : 4 * group + 4].reshape(128, WIDE)
        turned = jnp.transpose(flat)
        around = jnp.concatenate([turned[WIDE - margin :], turned[0 : COLS + margin]], axis=0)
        spread(around, turn_ref, a0_ref, group, zero)

    for group in range(8):
        turn(group)
    for layer, refs in enumerate(
        (
            (a0_ref, w1_ref, b1_ref, a1_ref, None),
            (a1_ref, w2_ref, b2_ref, a2_ref, mask2_ref),
            (a2_ref, w3_ref, b3_ref, a3_ref, mask3_ref),
        )
    ):
        sea = sea_ref if first else None
        skip = MARGINS[0] - margin
        conv_layer(refs, sum_ref, sea, work_ref, zero, layer, 7 - layer, skip)
    left = margin - HALO
    count = COLS + 2 * left
    lhs = jnp.concatenate([a3_ref[group, 0:count, :] for group in range(5)], axis=1)
    found = jnp.dot(lhs, w4_ref[...], preferred_element_type=F32)
    around = [found[left:], jnp.zeros((WIDE - count, 256), F32)]
    if left:
        around.append(found[:left])
    raw_ref[...] = jnp.transpose(jnp.concatenate(around, axis=0)).reshape(ROWS, 16, WIDE)

    def shifted_difference(field):
        return (pltpu.roll(field, WIDE - 1, 2) - pltpu.roll(field, 1, 2)) * 0.5

    rows = ROWS + 2
    low = HALO - 1
    zonal = state_ref[low : low + rows, 0:8, :]
    merid_above = state_ref[low + 1 : low + 1 + rows, 8:16, :]
    merid_below = state_ref[low - 1 : low - 1 + rows, 8:16, :]
    divergence = shifted_difference(zonal) + (merid_above - merid_below) * 0.5
    thickness = state_ref[low : low + rows, 16:24, :]
    h_new = (thickness - TIME_STEP * divergence) * wet_ref[low : low + rows]
    level = lax.broadcasted_iota(jnp.int32, (1, 8, 1), 1)
    pressure = None
    for other in range(LEVELS):
        weight = 0.5 + 0.1 * jnp.minimum(level, other).astype(F32)
        term = weight * h_new[:, other : other + 1, :]
        pressure = term if pressure is None else pressure + term
    grad_x = shifted_difference(pressure[1:-1])
    grad_y = (pressure[2:] - pressure[:-2]) * 0.5
    wet = wet_ref[HALO : HALO + ROWS]
    zonal_mid = state_ref[HALO : HALO + ROWS, 0:8, :]
    merid_mid = state_ref[HALO : HALO + ROWS, 8:16, :]
    global_row = start_ref[0] + lax.broadcasted_iota(jnp.int32, (ROWS, 8, WIDE), 0)
    coriolis = 0.3 + 0.5 * global_row.astype(F32) / 512.0
    raw_zonal = raw_ref[:, 0:8, :]
    raw_merid = raw_ref[:, 8:16, :]
    zonal_new = (
        zonal_mid + TIME_STEP * (-grad_x + coriolis * merid_mid - DRAG * zonal_mid + raw_zonal)
    ) * wet
    merid_new = (
        merid_mid + TIME_STEP * (-grad_y - coriolis * zonal_mid - DRAG * merid_mid + raw_merid)
    ) * wet
    new_ref[:, 0:8, :] = zonal_new
    new_ref[:, 8:16, :] = merid_new
    new_ref[:, 16:24, :] = h_new[1:-1]
    if last:
        raw_out_ref[...] = raw_ref[...]
    else:
        flat = new_ref[...].reshape(ROWS * 24, WIDE)
        send_down_ref[...] = pack_rows(flat[0 : HALO * 24]).astype(BF16)
        send_up_ref[...] = pack_rows(flat[(ROWS - HALO) * 24 :]).astype(BF16)

    def lanes_of(field):
        by_column = jnp.sum(field, axis=0)
        return by_column[:, 0:128] + by_column[:, 128:256]

    columns = jnp.concatenate(
        [
            lanes_of(raw_zonal * wet),
            lanes_of(raw_merid * wet),
            lanes_of(wet),
            jnp.zeros((104, 128), F32),
        ],
        axis=0,
    )
    row = jnp.sum(jnp.transpose(columns), axis=0, keepdims=True)
    pay_ref[...] = jnp.broadcast_to(row, (128, 128))


def ocean_network_step(step, args):
    first, last = step == 0, step == STEPS - 1
    span = COLS + 2 * MARGINS[step]
    outs = [
        jax.ShapeDtypeStruct((ROWS, 24, WIDE), F32),
        jax.ShapeDtypeStruct((128, 128), F32),
    ]
    if first:
        outs.append(jax.ShapeDtypeStruct((EXT_ROWS, LEVELS, WIDE), F32))
        outs.append(jax.ShapeDtypeStruct((6, span, 256), F32))
        outs.append(jax.ShapeDtypeStruct((5, span, 128), F32))
    if last:
        outs.append(jax.ShapeDtypeStruct((ROWS, 16, WIDE), F32))
    else:
        outs += [jax.ShapeDtypeStruct((HALO * 30, COLS), BF16)] * 2
    vmem = pl.BlockSpec(memory_space=pltpu.VMEM)
    return pl.pallas_call(
        functools.partial(step_kernel, step=step),
        out_shape=outs,
        in_specs=[pl.BlockSpec(memory_space=pltpu.SMEM)] + [vmem] * (len(args) - 1),
        out_specs=[vmem] * len(outs),
        scratch_shapes=[
            pltpu.VMEM((EXT_ROWS, 32, WIDE), F32),
            pltpu.VMEM((8, span, 5 * 128), BF16),
            pltpu.VMEM((7, span, 5 * 512), BF16),
            pltpu.VMEM((6, span, 5 * 256), BF16),
            pltpu.VMEM((5, span, 5 * 128), BF16),
            pltpu.VMEM((4, span + 8, 128), F32),
            pltpu.VMEM((ROWS, 16, WIDE), F32),
            pltpu.VMEM((2, span, 128), BF16),
            pltpu.VMEM((span, 512), F32),
            pltpu.VMEM((1, span + 8, 128), F32),
        ]
        + ([pltpu.VMEM((WIDE + 8, 128), F32)] if first else []),
        compiler_params=pltpu.CompilerParams(vmem_limit_bytes=32 * 2**20),
        name=f"step_{step}",
    )(*args)


def finish_kernel(recv_ref, state_ref, raw_ref, wet_ref, final_ref, forcing_ref, work_ref):
    zonal_mean, merid_mean = device_means(recv_ref[...])
    wet = wet_ref[HALO : HALO + ROWS, :, 0:COLS]
    zonal_mean = jnp.concatenate([zonal_mean] * 2, axis=1)[None]
    merid_mean = jnp.concatenate([merid_mean] * 2, axis=1)[None]
    work_ref[:, 0:8, :] = (raw_ref[:, 0:8, 0:COLS] - zonal_mean) * wet
    work_ref[:, 8:16, :] = (raw_ref[:, 8:16, 0:COLS] - merid_mean) * wet
    for channel in range(16):
        forcing_ref[channel] = work_ref[:, channel, :]
    work_ref[:, 0:8, :] = state_ref[:, 0:8, 0:COLS] - TIME_STEP * zonal_mean * wet
    work_ref[:, 8:16, :] = state_ref[:, 8:16, 0:COLS] - TIME_STEP * merid_mean * wet
    for channel in range(16):
        final_ref[channel] = work_ref[:, channel, :]
    for channel in range(16, 24):
        final_ref[channel] = state_ref[:, channel, 0:COLS]


def finish(received, state, raw, wet):
    return pl.pallas_call(
        finish_kernel,
        out_shape=[
            jax.ShapeDtypeStruct((24, ROWS, COLS), F32),
            jax.ShapeDtypeStruct((16, ROWS, COLS), F32),
        ],
        scratch_shapes=[pltpu.VMEM((ROWS, 16, COLS), F32)],
        compiler_params=pltpu.CompilerParams(vmem_limit_bytes=8 * 2**20),
        name="finish",
    )(received, state, raw, wet)


def both_ways(axis, up, down):
    count = lax.axis_size(axis)
    forward = [(i, i + 1) for i in range(count - 1)]
    backward = [(target, source) for source, target in forward]
    return lax.ppermute(up, axis, forward), lax.ppermute(down, axis, backward)


def local(
    ocean_state,
    land_mask,
    layer_count,
    conv1_weight,
    conv1_bias,
    conv2_weight,
    conv2_bias,
    conv3_weight,
    conv3_bias,
    conv4_weight,
):
    state, send_left, send_right = prepare(ocean_state, land_mask, layer_count)
    left, right = both_ways("sec", send_right, send_left)
    weights = banded(
        [conv1_weight, conv2_weight, conv3_weight, conv4_weight],
        [conv1_bias, conv2_bias, conv3_bias],
        send_left,
    )
    state, send_up, send_down = pack(state, left, right)
    halos = both_ways("lat", send_up, send_down)

    start = (lax.axis_index("lat") * ROWS).astype(jnp.int32)
    start = jnp.stack([start, jnp.zeros((), jnp.int32)])
    extras = []
    for step in range(STEPS):
        results = ocean_network_step(step, [start, state, *halos, *extras, *weights])
        state = results[0]
        if step == 0:
            wet, *masks = results[2:5]
        if step < STEPS - 1:
            halos = both_ways("lat", results[-2], results[-1])
        received = lax.all_to_all(results[1], ("sec", "lat"), 0, 0)
        extras = [received, wet, *masks]
    return finish(received, state, results[2], wet)


def solution(mesh):
    return jax.shard_map(
        local,
        mesh=mesh,
        in_specs=(
            P(None, "lat", "sec"),
            P("lat", "sec"),
            P("lat", "sec"),
            P(),
            P(),
            P(),
            P(),
            P(),
            P(),
            P(),
        ),
        out_specs=(P(None, "lat", "sec"), P(None, "lat", "sec")),
        check_vma=False,
    )
```

```python
import functools

import jax
import jax.numpy as jnp
from jax import lax
from jax.experimental import pallas as pl
from jax.experimental.pallas import tpu as pltpu
from jax.sharding import PartitionSpec as P

LEVELS = 8
STEPS = 4
HALO = 8
TIME_STEP = 0.3
DRAG = 0.05
ROWS = 16
COLS = 256
EXT_ROWS = ROWS + 2 * HALO
WIDE = COLS + 128
SIDE = 64
MARGINS = tuple(HALO * (STEPS - step) for step in range(STEPS))
LAND_OFFSET = -(2.0**24)
PADDED = (32, 128, 64, 32)
F32 = jnp.float32
BF16 = jnp.bfloat16


def banded_kernel(*refs):
    sources, band_refs, row_refs = refs[:5], refs[6:10], refs[10:13]
    copies, (flat_ref, turned_ref, sems) = refs[13:18], refs[18:]
    fetch = [
        pltpu.make_async_copy(source, copy, sems.at[index])
        for index, (source, copy) in enumerate(zip(sources, copies))
    ]
    for one in fetch:
        one.start()
    for one in fetch:
        one.wait()
    weight_refs, bias_ref = copies[:4], copies[4]
    for layer in range(4):
        weight_ref, band_ref = weight_refs[layer], band_refs[layer]
        turned_already = layer == 0
        out_width = weight_ref.shape[2 if turned_already else 1]
        in_width = weight_ref.shape[1 if turned_already else 2] // 5
        in_pad = PADDED[layer]
        groups = band_ref.shape[0] // (20 * in_pad)
        out_rows = band_ref.shape[1] // out_width
        wide = -(-5 * in_width // 128) * 128
        flat_ref[...] = jnp.zeros(flat_ref.shape, F32)
        for offset in range(5):
            if turned_already:
                turned_ref[offset, 0 : 5 * in_width, 0:out_width] = weight_ref[offset].astype(F32)
                continue
            flat_ref[0:out_width, 0 : 5 * in_width] = weight_ref[offset].astype(F32)
            turned_ref[offset, 0:wide, :] = jnp.transpose(flat_ref[:, 0:wide])
        extra = in_pad - in_width
        for group in range(groups):
            for shift in range(5):
                for row in range(4):
                    parts = []
                    for out_row in range(out_rows):
                        offset = 4 * group + row - out_row
                        if not 0 <= offset < 5:
                            parts.append(jnp.zeros((in_pad, out_width), F32))
                            continue
                        part = turned_ref[
                            offset, shift * in_width : (shift + 1) * in_width, 0:out_width
                        ]
                        if extra:
                            pad = jnp.zeros((extra, out_width), F32)
                            if layer == 0 and offset == 2 and shift == 2:
                                first = lax.broadcasted_iota(jnp.int32, pad.shape, 0) == 0
                                pad = jnp.where(first, LAND_OFFSET, 0.0)
                            part = jnp.concatenate([part, pad], axis=0)
                        parts.append(part)
                    base = ((group * 5 + shift) * 4 + row) * in_pad
                    band_ref[base : base + in_pad, :] = jnp.concatenate(parts, axis=1).astype(BF16)
    begin = 0
    for row_ref in row_refs:
        width = row_ref.shape[1] // 4
        row_ref[...] = jnp.concatenate([bias_ref[:, begin : begin + width]] * 4, axis=1)
        begin += width


def banded(weights, biases, after):
    shapes = [(1280, 512), (5120, 256), (2560, 128), (3200, 256)]
    outs = [jax.ShapeDtypeStruct(shape, BF16) for shape in shapes]
    outs += [jax.ShapeDtypeStruct((1, width), F32) for width in (512, 256, 128)]
    first, *others = weights
    args = [first.transpose(0, 2, 1), *others, jnp.concatenate(biases)[None]]
    return pl.pallas_call(
        banded_kernel,
        out_shape=outs,
        in_specs=[pl.BlockSpec(memory_space=pltpu.HBM)] * 5 + [pl.BlockSpec(memory_space=pl.ANY)],
        scratch_shapes=[pltpu.VMEM(arg.shape, arg.dtype) for arg in args]
        + [
            pltpu.VMEM((128, 640), F32),
            pltpu.VMEM((5, 640, 128), F32),
            pltpu.SemaphoreType.DMA((5,)),
        ],
        compiler_params=small_params(),
        name="banded",
    )(*args, after)


def lanes_between(shape, low, high):
    lane = lax.broadcasted_iota(jnp.int32, shape, 1)
    return (lane >= low) & (lane < high)


def fold_edge(tile, low):
    height = tile.shape[0] // 4
    folded = tile[0:height]
    for part in range(1, 4):
        moved = pltpu.roll(tile[part * height : (part + 1) * height], 32 * part, 1)
        begin = (low + 32 * part) % 128
        folded = jnp.where(lanes_between(moved.shape, begin, begin + 32), moved, folded)
    return folded


def unfold_edge(folded):
    parts = [folded] + [pltpu.roll(folded, 128 - 32 * part, 1) for part in range(1, 4)]
    return jnp.concatenate(parts, axis=0)


def fold_sides(sides):
    height = sides.shape[0] // 2
    moved = pltpu.roll(sides[height:], 64, 1)
    both = jnp.where(lanes_between(moved.shape, 32, 96), moved, sides[:height])
    return jnp.concatenate([both[: height // 2], both[height // 2 :]], axis=1)


def unfold_sides(folded):
    both = jnp.concatenate([folded[:, 0:128], folded[:, 128:256]], axis=0)
    return jnp.concatenate([both, pltpu.roll(both, 64, 1)], axis=0)


def pack_rows(flat):
    return jnp.concatenate([flat[:, 0:COLS], fold_sides(flat[:, COLS:])], axis=0)


def unpack_rows(packed, state_ref, low):
    height = HALO * 24
    fields = packed[0 : height + height // 4].astype(F32)
    state_ref[low : low + HALO, 0:24, 0:COLS] = fields[0:height].reshape(HALO, 24, COLS)
    state_ref[low : low + HALO, 0:24, COLS:WIDE] = unfold_sides(fields[height:]).reshape(
        HALO, 24, 128
    )


def prepare_kernel(*refs):
    sources, (own_ref, left_ref, right_ref), copies, sems = refs[:2], refs[2:5], refs[5:7], refs[7]
    fetch = [
        pltpu.make_async_copy(source, copy, sems.at[index])
        for index, (source, copy) in enumerate(zip(sources, copies))
    ]
    for one in fetch:
        one.start()
    for one in fetch:
        one.wait()
    state_ref, levels_ref = copies
    levels = levels_ref[...]
    own_ref[:, 24:32, :] = jnp.zeros((ROWS, 8, COLS), F32)
    own_ref[:, 24, :] = levels.astype(F32)
    for channel in range(24):
        wet = jnp.where(levels > channel % LEVELS, 1.0, 0.0)
        own_ref[:, channel, :] = state_ref[channel] * wet
    flat = own_ref[...].reshape(ROWS * 32, COLS)
    left_ref[...] = fold_edge(flat[:, 0:128], 0).astype(BF16)
    right_ref[...] = fold_edge(flat[:, COLS - 128 :], 96).astype(BF16)


def small_params():
    return pltpu.CompilerParams(vmem_limit_bytes=8 * 2**20)


def prepare(*args):
    return pl.pallas_call(
        prepare_kernel,
        out_shape=[jax.ShapeDtypeStruct((ROWS, 32, COLS), F32)]
        + [jax.ShapeDtypeStruct((ROWS * 8, 128), BF16)] * 2,
        in_specs=[pl.BlockSpec(memory_space=pltpu.HBM)] * 2,
        scratch_shapes=[pltpu.VMEM(arg.shape, arg.dtype) for arg in args]
        + [pltpu.SemaphoreType.DMA((2,))],
        compiler_params=small_params(),
        name="prepare",
    )(*args)


def pack_kernel(own_ref, left_ref, right_ref, wide_ref, up_ref, down_ref):
    right = unfold_edge(right_ref[...].astype(F32))
    left = unfold_edge(left_ref[...].astype(F32))
    sides = jnp.where(lanes_between(left.shape, 0, SIDE), right, left)
    wide_ref[:, :, 0:COLS] = own_ref[...]
    wide_ref[:, :, COLS:WIDE] = sides.reshape(ROWS, 32, 128)
    for low, out_ref in ((0, down_ref), (ROWS - HALO, up_ref)):
        fields = wide_ref[low : low + HALO, 0:24, :].reshape(HALO * 24, WIDE)
        levels = wide_ref[low : low + HALO, 24, :]
        rest = jnp.concatenate([levels[:, COLS:], jnp.zeros((HALO, 128), F32)], axis=1)
        out_ref[...] = jnp.concatenate(
            [pack_rows(fields), levels[:, 0:COLS], rest], axis=0
        ).astype(BF16)


def pack(own, left, right):
    return pl.pallas_call(
        pack_kernel,
        out_shape=[jax.ShapeDtypeStruct((ROWS, 32, WIDE), F32)]
        + [jax.ShapeDtypeStruct((HALO * 32, COLS), BF16)] * 2,
        compiler_params=small_params(),
        name="pack",
    )(own, left, right)


def spread(value, work_ref, out_ref, group, zero):
    span, width = value.shape
    out_ref[group, :, 0:width] = value.astype(BF16)
    for tile in range(width // 128):
        work_ref[tile, 0:span, :] = value[:, 128 * tile : 128 * tile + 128]
    for shift in range(1, 5):
        for tile in range(width // 128):
            base = shift * width + 128 * tile
            out_ref[group, :, base : base + 128] = work_ref[
                tile, pl.ds(zero + shift, span), :
            ].astype(BF16)


def conv_layer(refs, raw_ref, sea_ref, work_ref, zero, layer, groups, skip):
    in_ref, weight_ref, bias_ref, out_ref, mask_ref = refs
    span = in_ref.shape[1]
    width = weight_ref.shape[1]

    def activate(group):
        half = 0.5 * (raw_ref[:, 0:width] + bias_ref[...])
        value = half + half * jnp.tanh(half)
        if layer and sea_ref is not None:
            row_of = lax.broadcasted_iota(jnp.int32, (128, width), 0)
            lane_of = lax.broadcasted_iota(jnp.int32, (128, width), 1)
            wanted = 4 * group + 2 * (layer + 1) + lane_of // (width // 4)
            pick = jnp.where(row_of == wanted, 1.0, 0.0).astype(BF16)
            mask = jnp.dot(sea_ref[layer - 1], pick, preferred_element_type=F32)
            mask_ref[group] = mask
            value = value * mask
        elif layer:
            value = value * mask_ref[group, skip : skip + span, :]
        spread(value, work_ref, out_ref, group, zero)

    def body(group, carry):
        activate(jnp.maximum(group - 1, 0))
        lhs = jnp.concatenate([in_ref[group], in_ref[group + 1]], axis=1)
        raw_ref[:, 0:width] = jnp.dot(lhs, weight_ref[...], preferred_element_type=F32)
        return carry

    lax.fori_loop(0, groups, body, 0)
    activate(groups - 1)


def device_means(received):
    total = jnp.sum(received, axis=0, keepdims=True)
    column = jnp.transpose(jnp.broadcast_to(total, (128, 128)))
    counts = jnp.maximum(column[16:24], 1.0)
    return column[0:8] / counts, column[8:16] / counts


def step_kernel(*refs, step):
    first, last = step == 0, step == STEPS - 1
    margin = MARGINS[step]
    span = COLS + 2 * margin
    refs = list(refs)
    start_ref = refs.pop(0)
    own_ref, top_ref, bottom_ref = refs[:3]
    refs = refs[3:]
    if not first:
        recv_ref, wet_ref, mask2_ref, mask3_ref = refs[:4]
        refs = refs[4:]
    w1_ref, w2_ref, w3_ref, w4_ref, b1_ref, b2_ref, b3_ref, new_ref, pay_ref = refs[:9]
    refs = refs[9:]
    if first:
        wet_ref, mask2_ref, mask3_ref = refs[:3]
        refs = refs[3:]
    if last:
        raw_out_ref = refs.pop(0)
    else:
        send_up_ref, send_down_ref = refs[:2]
        refs = refs[2:]
    state_ref, a0_ref, a1_ref, a2_ref, a3_ref, work_ref, raw_ref, sea_ref, sum_ref = refs[:9]
    turn_ref = refs[9]
    sea_turned_ref = refs[10] if first else None
    zero = start_ref[0] // 65536

    halves = ((top_ref, 0), (bottom_ref, HALO + ROWS))
    for packed_ref, low in halves:
        unpack_rows(packed_ref[...], state_ref, low)
    if first:
        state_ref[HALO : HALO + ROWS] = own_ref[...]
        for packed_ref, low in halves:
            levels = packed_ref[HALO * 30 :, :].astype(F32)
            state_ref[low : low + HALO, 24, 0:COLS] = levels[0:HALO]
            state_ref[low : low + HALO, 24, COLS:WIDE] = levels[HALO:, 0:128]
        levels = jnp.broadcast_to(state_ref[:, 24:25, :], (EXT_ROWS, 8, WIDE))
        level_of = lax.broadcasted_iota(jnp.int32, levels.shape, 1).astype(F32)
        wet_ref[...] = jnp.where(level_of < levels, 1.0, 0.0)
        by_row = jnp.where(state_ref[:, 24, :] > 0.0, 1.0, 0.0)
        turned = jnp.transpose(
            jnp.concatenate([by_row, jnp.zeros((128 - EXT_ROWS, WIDE), F32)], axis=0)
        )
        sea_turned_ref[0:SIDE, :] = turned[WIDE - SIDE :]
        sea_turned_ref[SIDE:WIDE, :] = turned[0 : WIDE - SIDE]
        sea_turned_ref[WIDE:, :] = jnp.zeros((8, 128), F32)
    else:
        state_ref[HALO : HALO + ROWS, 0:24, :] = own_ref[...]
        zonal_mean, merid_mean = device_means(recv_ref[...])
        for base, mean in ((0, zonal_mean), (8, merid_mean)):
            scaled = jnp.concatenate([TIME_STEP * mean] * 3, axis=1)
            state_ref[:, base : base + 8, :] = (
                state_ref[:, base : base + 8, :] - scaled[None] * wet_ref[...]
            )
    first_channel = lax.broadcasted_iota(jnp.int32, (EXT_ROWS, 8, WIDE), 1) == 0
    state_ref[:, 24:32, :] = jnp.where(first_channel, 1.0 - wet_ref[...], 0.0)
    for layer in (1, 2) if first else ():
        begin = SIDE - margin + 2 * (layer + 1)
        sea_ref[layer - 1] = sea_turned_ref[begin : begin + span, :].astype(BF16)

    work_ref[:, span:, :] = jnp.zeros((4, 8, 128), F32)
    turn_ref[:, span:, :] = jnp.zeros((1, 8, 128), F32)

    def turn(group):
        flat = state_ref[4 * group : 4 * group + 4].reshape(128, WIDE)
        turned = jnp.transpose(flat)
        around = jnp.concatenate([turned[WIDE - margin :], turned[0 : COLS + margin]], axis=0)
        spread(around, turn_ref, a0_ref, group, zero)

    for group in range(8):
        turn(group)
    for layer, refs in enumerate(
        (
            (a0_ref, w1_ref, b1_ref, a1_ref, None),
            (a1_ref, w2_ref, b2_ref, a2_ref, mask2_ref),
            (a2_ref, w3_ref, b3_ref, a3_ref, mask3_ref),
        )
    ):
        sea = sea_ref if first else None
        skip = MARGINS[0] - margin
        conv_layer(refs, sum_ref, sea, work_ref, zero, layer, 7 - layer, skip)
    left = margin - HALO
    count = COLS + 2 * left
    lhs = jnp.concatenate([a3_ref[group, 0:count, :] for group in range(5)], axis=1)
    found = jnp.dot(lhs, w4_ref[...], preferred_element_type=F32)
    around = [found[left:], jnp.zeros((WIDE - count, 256), F32)]
    if left:
        around.append(found[:left])
    raw_ref[...] = jnp.transpose(jnp.concatenate(around, axis=0)).reshape(ROWS, 16, WIDE)

    def shifted_difference(field):
        return (pltpu.roll(field, WIDE - 1, 2) - pltpu.roll(field, 1, 2)) * 0.5

    rows = ROWS + 2
    low = HALO - 1
    zonal = state_ref[low : low + rows, 0:8, :]
    merid_above = state_ref[low + 1 : low + 1 + rows, 8:16, :]
    merid_below = state_ref[low - 1 : low - 1 + rows, 8:16, :]
    divergence = shifted_difference(zonal) + (merid_above - merid_below) * 0.5
    thickness = state_ref[low : low + rows, 16:24, :]
    h_new = (thickness - TIME_STEP * divergence) * wet_ref[low : low + rows]
    level = lax.broadcasted_iota(jnp.int32, (1, 8, 1), 1)
    pressure = None
    for other in range(LEVELS):
        weight = 0.5 + 0.1 * jnp.minimum(level, other).astype(F32)
        term = weight * h_new[:, other : other + 1, :]
        pressure = term if pressure is None else pressure + term
    grad_x = shifted_difference(pressure[1:-1])
    grad_y = (pressure[2:] - pressure[:-2]) * 0.5
    wet = wet_ref[HALO : HALO + ROWS]
    zonal_mid = state_ref[HALO : HALO + ROWS, 0:8, :]
    merid_mid = state_ref[HALO : HALO + ROWS, 8:16, :]
    global_row = start_ref[0] + lax.broadcasted_iota(jnp.int32, (ROWS, 8, WIDE), 0)
    coriolis = 0.3 + 0.5 * global_row.astype(F32) / 512.0
    raw_zonal = raw_ref[:, 0:8, :]
    raw_merid = raw_ref[:, 8:16, :]
    zonal_new = (
        zonal_mid + TIME_STEP * (-grad_x + coriolis * merid_mid - DRAG * zonal_mid + raw_zonal)
    ) * wet
    merid_new = (
        merid_mid + TIME_STEP * (-grad_y - coriolis * zonal_mid - DRAG * merid_mid + raw_merid)
    ) * wet
    new_ref[:, 0:8, :] = zonal_new
    new_ref[:, 8:16, :] = merid_new
    new_ref[:, 16:24, :] = h_new[1:-1]
    if last:
        raw_out_ref[...] = raw_ref[...]
    else:
        flat = new_ref[...].reshape(ROWS * 24, WIDE)
        send_down_ref[...] = pack_rows(flat[0 : HALO * 24]).astype(BF16)
        send_up_ref[...] = pack_rows(flat[(ROWS - HALO) * 24 :]).astype(BF16)

    def lanes_of(field):
        by_column = jnp.sum(field, axis=0)
        return by_column[:, 0:128] + by_column[:, 128:256]

    columns = jnp.concatenate(
        [
            lanes_of(raw_zonal * wet),
            lanes_of(raw_merid * wet),
            lanes_of(wet),
            jnp.zeros((104, 128), F32),
        ],
        axis=0,
    )
    row = jnp.sum(jnp.transpose(columns), axis=0, keepdims=True)
    pay_ref[...] = jnp.broadcast_to(row, (128, 128))


def ocean_network_step(step, args):
    first, last = step == 0, step == STEPS - 1
    span = COLS + 2 * MARGINS[step]
    outs = [
        jax.ShapeDtypeStruct((ROWS, 24, WIDE), F32),
        jax.ShapeDtypeStruct((128, 128), F32),
    ]
    if first:
        outs.append(jax.ShapeDtypeStruct((EXT_ROWS, LEVELS, WIDE), F32))
        outs.append(jax.ShapeDtypeStruct((6, span, 256), F32))
        outs.append(jax.ShapeDtypeStruct((5, span, 128), F32))
    if last:
        outs.append(jax.ShapeDtypeStruct((ROWS, 16, WIDE), F32))
    else:
        outs += [jax.ShapeDtypeStruct((HALO * 30, COLS), BF16)] * 2
    vmem = pl.BlockSpec(memory_space=pltpu.VMEM)
    return pl.pallas_call(
        functools.partial(step_kernel, step=step),
        out_shape=outs,
        in_specs=[pl.BlockSpec(memory_space=pltpu.SMEM)] + [vmem] * (len(args) - 1),
        out_specs=[vmem] * len(outs),
        scratch_shapes=[
            pltpu.VMEM((EXT_ROWS, 32, WIDE), F32),
            pltpu.VMEM((8, span, 5 * 128), BF16),
            pltpu.VMEM((7, span, 5 * 512), BF16),
            pltpu.VMEM((6, span, 5 * 256), BF16),
            pltpu.VMEM((5, span, 5 * 128), BF16),
            pltpu.VMEM((4, span + 8, 128), F32),
            pltpu.VMEM((ROWS, 16, WIDE), F32),
            pltpu.VMEM((2, span, 128), BF16),
            pltpu.VMEM((span, 512), F32),
            pltpu.VMEM((1, span + 8, 128), F32),
        ]
        + ([pltpu.VMEM((WIDE + 8, 128), F32)] if first else []),
        compiler_params=pltpu.CompilerParams(vmem_limit_bytes=32 * 2**20),
        name=f"step_{step}",
    )(*args)


def finish_kernel(recv_ref, state_ref, raw_ref, wet_ref, final_ref, forcing_ref, work_ref):
    zonal_mean, merid_mean = device_means(recv_ref[...])
    wet = wet_ref[HALO : HALO + ROWS, :, 0:COLS]
    zonal_mean = jnp.concatenate([zonal_mean] * 2, axis=1)[None]
    merid_mean = jnp.concatenate([merid_mean] * 2, axis=1)[None]
    work_ref[:, 0:8, :] = (raw_ref[:, 0:8, 0:COLS] - zonal_mean) * wet
    work_ref[:, 8:16, :] = (raw_ref[:, 8:16, 0:COLS] - merid_mean) * wet
    for channel in range(16):
        forcing_ref[channel] = work_ref[:, channel, :]
    work_ref[:, 0:8, :] = state_ref[:, 0:8, 0:COLS] - TIME_STEP * zonal_mean * wet
    work_ref[:, 8:16, :] = state_ref[:, 8:16, 0:COLS] - TIME_STEP * merid_mean * wet
    for channel in range(16):
        final_ref[channel] = work_ref[:, channel, :]
    for channel in range(16, 24):
        final_ref[channel] = state_ref[:, channel, 0:COLS]


def finish(received, state, raw, wet):
    return pl.pallas_call(
        finish_kernel,
        out_shape=[
            jax.ShapeDtypeStruct((24, ROWS, COLS), F32),
            jax.ShapeDtypeStruct((16, ROWS, COLS), F32),
        ],
        scratch_shapes=[pltpu.VMEM((ROWS, 16, COLS), F32)],
        compiler_params=pltpu.CompilerParams(vmem_limit_bytes=8 * 2**20),
        name="finish",
    )(received, state, raw, wet)


def both_ways(axis, up, down):
    count = lax.axis_size(axis)
    forward = [(i, i + 1) for i in range(count - 1)]
    backward = [(target, source) for source, target in forward]
    return lax.ppermute(up, axis, forward), lax.ppermute(down, axis, backward)


def local(
    ocean_state,
    land_mask,
    layer_count,
    conv1_weight,
    conv1_bias,
    conv2_weight,
    conv2_bias,
    conv3_weight,
    conv3_bias,
    conv4_weight,
):
    state, send_left, send_right = prepare(ocean_state, land_mask * layer_count)
    left, right = both_ways("sec", send_right, send_left)
    weights = banded(
        [conv1_weight, conv2_weight, conv3_weight, conv4_weight],
        [conv1_bias, conv2_bias, conv3_bias],
        send_left,
    )
    state, send_up, send_down = pack(state, left, right)
    halos = both_ways("lat", send_up, send_down)

    start = (lax.axis_index("lat") * ROWS).astype(jnp.int32)[None]
    extras = []
    for step in range(STEPS):
        results = ocean_network_step(step, [start, state, *halos, *extras, *weights])
        state = results[0]
        if step == 0:
            wet, *masks = results[2:5]
        if step < STEPS - 1:
            halos = both_ways("lat", results[-2], results[-1])
        received = lax.all_to_all(results[1], ("sec", "lat"), 0, 0)
        extras = [received, wet, *masks]
    return finish(received, state, results[2], wet)


def solution(mesh):
    return jax.shard_map(
        local,
        mesh=mesh,
        in_specs=(
            P(None, "lat", "sec"),
            P("lat", "sec"),
            P("lat", "sec"),
            P(),
            P(),
            P(),
            P(),
            P(),
            P(),
            P(),
        ),
        out_specs=(P(None, "lat", "sec"), P(None, "lat", "sec")),
        check_vma=False,
    )
```
